32 devices in a mesh: groups: 2 (over x), patch: 16 (over z, y, core).
Axes of the slice: x: 2, y: 2, z: 4, core: 2. Of those that a mesh axis runs over, the one named last changes fastest.
Arguments:
- nodes: bfloat16 [10240, 512], P(('groups', 'patch')), parts along dimension 0, may hold values from -6 to 6
- edges: bfloat16 [49152, 512], P(('groups', 'patch')), parts along dimension 0, may hold values from -6 to 6
- node_cot: bfloat16 [10240, 512], P(('groups', 'patch')), parts along dimension 0, may hold values from -6 to 6
- edge_cot: bfloat16 [49152, 512], P(('groups', 'patch')), parts along dimension 0, may hold values from -6 to 6
- w_edge: bfloat16 [512, 512], replicated, may hold values from -0.15625 to 0.15625
- w_send: bfloat16 [512, 512], replicated, may hold values from -0.15625 to 0.15625
- w_recv: bfloat16 [512, 512], replicated, may hold values from -0.15625 to 0.15625
- edge_bias: float32 [512], replicated, may hold values from -3 to 3
- w_edge_out: bfloat16 [512, 512], replicated, may hold values from -0.25 to 0.25
- edge_out_bias: float32 [512], replicated, may hold values from -3 to 3
- edge_gain: float32 [512], replicated, may hold values from 0.25 to 1.75
- w_node: bfloat16 [512, 512], replicated, may hold values from -0.1875 to 0.1875
- w_agg: bfloat16 [512, 512], replicated, may hold values from -0.1875 to 0.1875
- node_bias: float32 [512], replicated, may hold values from -3 to 3
- w_node_out: bfloat16 [512, 512], replicated, may hold values from -0.25 to 0.25
- node_out_bias: float32 [512], replicated, may hold values from -3 to 3
- node_gain: float32 [512], replicated, may hold values from 0.25 to 1.75
- send_slots: int32 [24576], P('patch'), may hold values from 0 to 607, as said below
- recv_slots: int32 [24576], P('patch'), may hold values from 0 to 319
- neighbour_send_lists: int32 [64, 64], P('patch'), may hold values from 0 to 319
- coarse_rows: int32 [128], P('patch'), may hold values from 0 to 319, as said below
- far_lists: int32 [16, 16, 2], P('patch'), may hold values from 0 to 7
- block_count: int32 [16], P('patch'), may hold values from 6 to 12, as said below
Outputs:
- new_nodes: bfloat16 [10240, 512], P(('groups', 'patch')), parts along dimension 0
- new_edges: bfloat16 [49152, 512], P(('groups', 'patch')), parts along dimension 0
- node_grad: bfloat16 [10240, 512], P(('groups', 'patch')), parts along dimension 0
- edge_grad: bfloat16 [49152, 512], P(('groups', 'patch')), parts along dimension 0
The draws below stay inside these ranges and needn't reach their ends.
There are 2 independent parts, one for each index of `groups`. The reference program is written for one: setup_inputs(seed, part) draws one part's arguments, and reference() takes and returns one part's arrays. A program takes and returns all parts, laid end to end along the dimension named above; an argument that names none is the same for every part. Nothing has to cross between parts.
Inputs may be any that keep to these rules, and one draw needn't show every extreme that they name: `send_slots`: addresses below 320 are rows of the edge's own patch, the next 256 are neighbour slots, the last 16 * 2 are distant slots. `coarse_rows`: the 8 rows of one patch are distinct. `block_count`: some patches have all 12 blocks live in every draw.
All inputs are finite; a program needn't handle non-finite values.
Results may differ from the reference program's by a relative error of at most 0.013.
Values may be sent and summed in bfloat16 or wider, within the bound.
No kernel may reach another device: no remote copies, remote signals or barrier semaphores. Data moves between devices by JAX's collectives and lax.ppermute only.
A program may use at most 128 MiB of HBM per device.

```python
import jax
import jax.numpy as jnp
from jax import lax

D = 512
HID = 512
PATCH_NODES = 320
EDGE_BLOCKS = 12
BLOCK = 128
NEIGHBOUR_COUNT = 4
NEAR_SLOT_ROWS = 64
FAR_SLOT_ROWS = 2
COARSE_DEV = 8
NODES = 5120
EDGES_DEV = 1536
EDGE_SLOTS_ALL = 24576
N_PATCH = 16


def draw_send_slots(key, part):
    random_keys = jax.random.split(jax.random.fold_in(key, 11), 4)
    kind = jax.random.randint(random_keys[0], (EDGE_SLOTS_ALL,), 0, 20)
    local_rows = jax.random.randint(random_keys[1], (EDGE_SLOTS_ALL,), 0, PATCH_NODES)
    neighbour_rows = PATCH_NODES + jax.random.randint(random_keys[2], (EDGE_SLOTS_ALL,), 0, NEIGHBOUR_COUNT * NEAR_SLOT_ROWS)
    distant_rows = PATCH_NODES + NEIGHBOUR_COUNT * NEAR_SLOT_ROWS + jax.random.randint(random_keys[3], (EDGE_SLOTS_ALL,), 0, N_PATCH * FAR_SLOT_ROWS)
    return jnp.where(kind < 12, local_rows, jnp.where(kind < 17, neighbour_rows, distant_rows)).astype(jnp.int32)


def draw_coarse_rows(key, part):
    random_keys = jax.random.split(jax.random.fold_in(key, 23), N_PATCH)

    def choose(single):
        return jax.random.permutation(single, PATCH_NODES)[:COARSE_DEV]
    return jax.vmap(choose)(random_keys).reshape(-1).astype(jnp.int32)


def draw_block_count(key, part):
    random_keys = jax.random.split(jax.random.fold_in(key, 37), 2)
    lowest = max(1, EDGE_BLOCKS // 2)
    counts = jax.random.randint(random_keys[0], (N_PATCH,), lowest, EDGE_BLOCKS + 1)
    busiest = jax.random.permutation(random_keys[1], N_PATCH)[:3]
    return counts.at[busiest].set(EDGE_BLOCKS).astype(jnp.int32)


def place_ends(drawn, stream_key, low, top_value):
    shape = drawn.shape
    place = [jax.random.randint(jax.random.fold_in(stream_key, axis), (), 0, shape[axis]) for axis in range(len(shape))]
    drawn = drawn.at[tuple(place)].set(low)
    longest = shape.index(max(shape))
    place[longest] = (place[longest] + 1) % shape[longest]
    return drawn.at[tuple(place)].set(top_value)


def steps_of(stream_key, extent, shards, low, high):
    level = 1.0
    for dim, parts in shards:
        heights = jax.random.uniform(jax.random.fold_in(jax.random.fold_in(stream_key, 6), dim), (parts,), jnp.float32, low / len(shards), high / len(shards))
        level = level * jnp.repeat(jnp.exp(heights), extent[dim] // parts).reshape((-1,) + (1,) * (len(extent) - 1 - dim))
    return level


def gaussian(stream_key, dims, scale, bound, cuts=(), kind=jnp.bfloat16):
    values = scale * jax.random.normal(stream_key, dims, jnp.float32)
    if cuts:
        values = values * steps_of(stream_key, dims, cuts, -0.22, 0.18)
    return jnp.clip(values, -bound, bound).astype(kind)


def setup_inputs(seed: int = 0, part: int = 0) -> dict:
    keys = jax.random.split(jax.random.key(seed), 24)
    own_keys = jax.random.split(jax.random.fold_in(keys[23], part), 24)
    nodes = gaussian(own_keys[0], (NODES, D), 1.0, 6.0, ((0, 16),))
    edges = gaussian(own_keys[1], (EDGE_SLOTS_ALL, D), 1.0, 6.0, ((0, 16),))
    node_cot = gaussian(own_keys[2], (NODES, D), 1.0, 6.0, ((0, 16),))
    edge_cot = gaussian(own_keys[3], (EDGE_SLOTS_ALL, D), 1.0, 6.0, ((0, 16),))
    w_edge = gaussian(keys[4], (D, HID), (3 * D) ** -0.5, 0.15625)
    w_send = gaussian(keys[5], (D, HID), (3 * D) ** -0.5, 0.15625)
    w_recv = gaussian(keys[6], (D, HID), (3 * D) ** -0.5, 0.15625)
    edge_bias = gaussian(keys[7], (HID,), 0.5, 3.0, (), jnp.float32)
    w_edge_out = gaussian(keys[8], (HID, D), HID ** -0.5, 0.25)
    edge_out_bias = gaussian(keys[9], (D,), 0.5, 3.0, (), jnp.float32)
    edge_gain = jnp.clip(1.0 + 0.15 * jax.random.normal(keys[10], (D,), jnp.float32), 0.25, 1.75)
    w_node = gaussian(keys[11], (D, HID), (2 * D) ** -0.5, 0.1875)
    w_agg = gaussian(keys[12], (D, HID), (2 * D) ** -0.5, 0.1875)
    node_bias = gaussian(keys[13], (HID,), 0.5, 3.0, (), jnp.float32)
    w_node_out = gaussian(keys[14], (HID, D), HID ** -0.5, 0.25)
    node_out_bias = gaussian(keys[15], (D,), 0.5, 3.0, (), jnp.float32)
    node_gain = jnp.clip(1.0 + 0.15 * jax.random.normal(keys[16], (D,), jnp.float32), 0.25, 1.75)
    send_slots = draw_send_slots(jax.random.fold_in(keys[23], 71), part)
    recv_slots = place_ends(jax.random.randint(keys[18], (EDGE_SLOTS_ALL,), 0, PATCH_NODES), jax.random.fold_in(keys[18], 1), 0, PATCH_NODES - 1).astype(jnp.int32)
    neighbour_send_lists = place_ends(jax.random.randint(keys[19], (N_PATCH * NEIGHBOUR_COUNT, NEAR_SLOT_ROWS), 0, PATCH_NODES), jax.random.fold_in(keys[19], 1), 0, PATCH_NODES - 1).astype(jnp.int32)
    coarse_rows = draw_coarse_rows(jax.random.fold_in(keys[23], 71), part)
    far_lists = place_ends(jax.random.randint(keys[21], (N_PATCH, N_PATCH, FAR_SLOT_ROWS), 0, COARSE_DEV), jax.random.fold_in(keys[21], 1), 0, COARSE_DEV - 1).astype(jnp.int32)
    block_count = draw_block_count(jax.random.fold_in(keys[23], 71), part)
    return dict(nodes=nodes, edges=edges, node_cot=node_cot, edge_cot=edge_cot, w_edge=w_edge, w_send=w_send, w_recv=w_recv, edge_bias=edge_bias, w_edge_out=w_edge_out, edge_out_bias=edge_out_bias, edge_gain=edge_gain, w_node=w_node, w_agg=w_agg, node_bias=node_bias, w_node_out=w_node_out, node_out_bias=node_out_bias, node_gain=node_gain, send_slots=send_slots, recv_slots=recv_slots, neighbour_send_lists=neighbour_send_lists, coarse_rows=coarse_rows, far_lists=far_lists, block_count=block_count)


def normalize(values):
    center = values - lax.optimization_barrier(jnp.mean(values, axis=-1, keepdims=True))
    spread = lax.optimization_barrier(jnp.mean(center * center, axis=-1, keepdims=True))
    return center * lax.rsqrt(spread + 1e-05)

def layer(node_rows, edge_rows, table, sending_patch, receiver, live, params):
    w_edge, w_send, w_recv, edge_bias, w_edge_out, edge_out_bias, edge_gain, w_node, w_agg, node_bias, w_node_out, node_out_bias, node_gain = params
    send_rows = jnp.take(table, sending_patch, axis=0).astype(jnp.bfloat16)
    recv_rows = jnp.take(node_rows, receiver, axis=0).astype(jnp.bfloat16)
    pre_edge = jnp.dot(edge_rows.astype(jnp.bfloat16), w_edge, preferred_element_type=jnp.float32)
    pre_edge = pre_edge + jnp.dot(send_rows, w_send, preferred_element_type=jnp.float32)
    pre_edge = pre_edge + jnp.dot(recv_rows, w_recv, preferred_element_type=jnp.float32) + edge_bias
    edge_hidden = jax.nn.silu(pre_edge).astype(jnp.bfloat16)
    edge_out = jnp.dot(edge_hidden, w_edge_out, preferred_element_type=jnp.float32) + edge_out_bias
    message = live[:, None] * edge_gain * normalize(edge_out)
    new_edges = edge_rows + message
    sent_message = message.astype(jnp.bfloat16)
    aggregate = jax.ops.segment_sum(sent_message.astype(jnp.float32), receiver, num_segments=node_rows.shape[0])
    aggregate = aggregate.astype(jnp.bfloat16)
    pre_node = jnp.dot(node_rows.astype(jnp.bfloat16), w_node, preferred_element_type=jnp.float32)
    pre_node = pre_node + jnp.dot(aggregate, w_agg, preferred_element_type=jnp.float32) + node_bias
    node_hidden = jax.nn.silu(pre_node).astype(jnp.bfloat16)
    node_out = jnp.dot(node_hidden, w_node_out, preferred_element_type=jnp.float32) + node_out_bias
    new_nodes = node_rows + node_gain * normalize(node_out)
    return (new_nodes, new_edges)

def reference(nodes, edges, node_cot, edge_cot, w_edge, w_send, w_recv, edge_bias, w_edge_out, edge_out_bias, edge_gain, w_node, w_agg, node_bias, w_node_out, node_out_bias, node_gain, send_slots, recv_slots, neighbour_send_lists, coarse_rows, far_lists, block_count):
    params = (w_edge, w_send, w_recv, edge_bias, w_edge_out, edge_out_bias, edge_gain, w_node, w_agg, node_bias, w_node_out, node_out_bias, node_gain)
    patch_count_total = N_PATCH
    position = jnp.arange(EDGE_SLOTS_ALL, dtype=jnp.int32)
    owner = position // EDGES_DEV
    row_address = send_slots
    home_node = owner * PATCH_NODES + row_address
    neighbour_patch = jnp.clip(row_address - PATCH_NODES, 0, NEIGHBOUR_COUNT * NEAR_SLOT_ROWS - 1)
    neighbour_offset = neighbour_patch // NEAR_SLOT_ROWS
    neighbour_slot = neighbour_patch % NEAR_SLOT_ROWS
    offset = (neighbour_offset // 2 + 1) * (1 - 2 * (neighbour_offset % 2))
    near_source = (owner - offset) % patch_count_total
    neighbour_node = near_source * PATCH_NODES + neighbour_send_lists[near_source * NEIGHBOUR_COUNT + neighbour_offset, neighbour_slot]
    distant_patch = jnp.clip(row_address - PATCH_NODES - NEIGHBOUR_COUNT * NEAR_SLOT_ROWS, 0, patch_count_total * FAR_SLOT_ROWS - 1)
    far_source = distant_patch // FAR_SLOT_ROWS
    far_slot = distant_patch % FAR_SLOT_ROWS
    coarse_index = far_lists[owner, far_source, far_slot]
    distant_node = far_source * PATCH_NODES + coarse_rows[far_source * COARSE_DEV + coarse_index]
    sending_patch = jnp.where(row_address < PATCH_NODES, home_node, jnp.where(row_address < PATCH_NODES + NEIGHBOUR_COUNT * NEAR_SLOT_ROWS, neighbour_node, distant_node)).astype(jnp.int32)
    receiver = (owner * PATCH_NODES + recv_slots).astype(jnp.int32)
    live = (position % EDGES_DEV // BLOCK < block_count[owner]).astype(jnp.float32)
    nodes_wide = nodes.astype(jnp.float32)
    edges_wide = edges.astype(jnp.float32)

    def forward(node_rows, edge_rows):
        return layer(node_rows, edge_rows, node_rows, sending_patch, receiver, live, params)
    (new_nodes, new_edges), pull = jax.vjp(forward, nodes_wide, edges_wide)
    node_grad, edge_grad = pull((node_cot.astype(jnp.float32), edge_cot.astype(jnp.float32)))
    return (new_nodes.astype(jnp.bfloat16), new_edges.astype(jnp.bfloat16), node_grad.astype(jnp.bfloat16), edge_grad.astype(jnp.bfloat16))
```

```python
import jax
import jax.numpy as jnp
from jax import lax
from jax.experimental import pallas as pl
from jax.experimental.pallas import tpu as pltpu
from jax.sharding import PartitionSpec as P

BLOCK = 128
LANES = 128
ROWS = 256
CHUNK = 32
EPS = 1e-05
BF = jnp.bfloat16
F32 = jnp.float32


def passed_along(value, axis, steps):
    count = lax.axis_size(axis)
    pairs = [(source, (source + steps) % count) for source in range(count)]
    return lax.ppermute(value, axis, pairs)


def mm(a, b):
    return lax.dot_general(a, b, (((1,), (0,)), ((), ())), preferred_element_type=F32)


def mm_t(a, b):
    return lax.dot_general(a, b, (((1,), (1,)), ((), ())), preferred_element_type=F32)


def mm_l(a, b):
    return lax.dot_general(a, b, (((0,), (0,)), ((), ())), preferred_element_type=F32)


def ones_where(mask):
    return jnp.where(mask, 1.0, 0.0).astype(BF)


def as_columns(row):
    return jnp.broadcast_to(row.astype(F32), (LANES, LANES)).T.astype(jnp.int32)


def lane_ids(tile):
    return lax.broadcasted_iota(jnp.int32, (LANES, LANES), 1) + tile * LANES


def own_pick(send, recv, own):
    sender = as_columns(jnp.where(send < own, send, -1))
    receiver = as_columns(recv + own)
    tiles = []
    for tile in range(2 * own // LANES):
        ids = lane_ids(tile)
        if (tile + 1) * LANES <= own:
            hit = sender == ids
        elif tile * LANES >= own:
            hit = receiver == ids
        else:
            hit = (sender == ids) | (receiver == ids)
        tiles.append(ones_where(hit))
    return jnp.concatenate(tiles, axis=1)


def own_pick_t(send, recv, own):
    sender = jnp.where(send < own, send, -1)
    ids = lax.broadcasted_iota(jnp.int32, (own, LANES), 0)
    return jnp.concatenate([ones_where(ids == sender), ones_where(ids == recv)], axis=0)


def remote_index(send, own, near, peers, shift):
    far = send - (own + near)
    far_index = near + (far & ((1 << shift) - 1)) * peers + (far >> shift)
    return jnp.where(send < own + near, send - own, far_index)


def pick(row, width):
    column = as_columns(row)
    return jnp.concatenate(
        [ones_where(column == lane_ids(tile)) for tile in range(width // LANES)], axis=1
    )


def pick_t(row, height):
    return ones_where(lax.broadcasted_iota(jnp.int32, (height, LANES), 0) == row)


def silu_parts(value):
    gate = 0.5 * jnp.tanh(0.5 * value) + 0.5
    hidden = value * gate
    slope = gate * (1.0 + value - hidden)
    return hidden, slope


def norm_parts(value):
    center = value - jnp.mean(value, axis=-1, keepdims=True)
    inverse = lax.rsqrt(jnp.mean(center * center, axis=-1, keepdims=True) + EPS)
    return center * inverse, inverse


def norm_back(grad, unit, inverse):
    first = jnp.mean(grad, axis=-1, keepdims=True)
    second = jnp.mean(grad * unit, axis=-1, keepdims=True)
    return inverse * (grad - first - unit * second)


def pack_kernel(nodes, lists, coarse, *outs):
    rows = nodes[...]
    own = rows.shape[0]
    steps, width = lists.shape
    ids = lax.broadcasted_iota(jnp.int32, (own, width), 0)
    for index in range(steps):
        hit = ones_where(ids == lists[index : index + 1, :])
        outs[index][...] = mm_l(hit, rows).astype(BF)
    count = coarse.shape[1]
    hit = ones_where(lax.broadcasted_iota(jnp.int32, (own, count), 0) == coarse[...])
    picked = mm_l(hit, rows).astype(BF)
    out = outs[steps]

    def put(index, carry):
        out[index] = picked
        return carry

    lax.fori_loop(0, out.shape[0], put, 0)


def local_kernel(nodes, edges, w_edge, w_send, w_recv, bias, send, recv, out, table):
    own = nodes.shape[0]
    rows = nodes[...]
    table[:own] = mm(rows, w_send[...]).astype(BF)
    table[own:] = mm(rows, w_recv[...]).astype(BF)
    parts = ROWS // LANES

    def step(index, carry):
        start = pl.multiple_of(index * ROWS, ROWS)
        hit = jnp.concatenate(
            [
                own_pick(
                    send[pl.ds(index * parts + part, 1), :],
                    recv[pl.ds(index * parts + part, 1), :],
                    own,
                )
                for part in range(parts)
            ],
            axis=0,
        )
        value = mm(edges[pl.ds(start, ROWS), :], w_edge[...]) + mm(hit, table[...]) + bias[...]
        out[pl.ds(start, ROWS), :] = value
        return carry

    lax.fori_loop(0, edges.shape[0] // ROWS, step, 0)


def main_kernel(
    shift,
    steps,
    count,
    *refs,
):
    (pre_in, edges, edge_cot, nodes, node_cot, send, recv, far_lists, coarse) = refs[:9]
    near = refs[9 : 9 + steps]
    (
        w_send,
        w_edge_out,
        edge_out_bias,
        edge_gain,
        w_node,
        w_agg,
        node_bias,
        w_node_out,
        node_out_bias,
        node_gain,
    ) = refs[9 + steps : 19 + steps]
    (new_nodes, new_edges, d_pre, d_node) = refs[19 + steps : 23 + steps]
    near_out = refs[23 + steps : 23 + 2 * steps]
    far_out = refs[23 + 2 * steps]
    (rows2, table2, slope, unit, inverse, agg, d_agg, sums2) = refs[24 + 2 * steps :]
    own = nodes.shape[0]
    width = nodes.shape[1]
    peers, far_width = far_lists.shape
    near_width = near[0].shape[0]
    near_rows = steps * near_width
    height = table2.shape[0]
    coarse_rows = coarse.shape[0] // peers
    parts = ROWS // LANES
    blocks = edges.shape[0] // ROWS
    live_count = count[0]

    far_ids = lax.broadcasted_iota(jnp.int32, (peers, coarse.shape[0]), 1)
    far_base = lax.broadcasted_iota(jnp.int32, (peers, coarse.shape[0]), 0) * coarse_rows
    far_hits = [
        ones_where(far_ids == far_base + far_lists[:, slot : slot + 1])
        for slot in range(far_width)
    ]
    rows2[...] = jnp.zeros(rows2.shape, BF)
    for index in range(steps):
        rows2[index * near_width : (index + 1) * near_width] = near[index][...]
    for slot in range(far_width):
        start = near_rows + slot * peers
        rows2[start : start + peers] = mm(far_hits[slot], coarse[...]).astype(BF)
    table2[...] = mm(rows2[...], w_send[...]).astype(BF)
    agg[...] = jnp.zeros(agg.shape, F32)

    def block_rows(ref, index, part):
        return ref[pl.ds(index * parts + part, 1), :]

    def ahead(index, carry):
        start = pl.multiple_of(index * ROWS, ROWS)
        hit = jnp.concatenate(
            [
                pick(remote_index(block_rows(send, index, part), own, near_rows, peers, shift), height)
                for part in range(parts)
            ],
            axis=0,
        )
        remote = mm(hit, table2[...])
        hidden = []
        for low in range(0, ROWS, CHUNK):
            here = pl.ds(start + low, CHUNK)
            value = pre_in[here, :] + remote[low : low + CHUNK]
            part_hidden, part_slope = silu_parts(value)
            slope[here, :] = part_slope
            hidden.append(part_hidden.astype(BF))
        out = mm(jnp.concatenate(hidden, axis=0), w_edge_out[...])
        sent = []
        for low in range(0, ROWS, CHUNK):
            here = pl.ds(start + low, CHUNK)
            live = jnp.where(index * parts + low // BLOCK < live_count, 1.0, 0.0).astype(F32)
            part_unit, part_inverse = norm_parts(out[low : low + CHUNK] + edge_out_bias[...])
            unit[here, :] = part_unit
            inverse[here, :] = part_inverse
            message = part_unit * (edge_gain[...] * live)
            new_edges[here, :] = (edges[here, :].astype(F32) + message).astype(BF)
            sent.append(message.astype(BF))
        hit_t = jnp.concatenate(
            [pick_t(block_rows(recv, index, part), own) for part in range(parts)], axis=1
        )
        agg[...] += mm(hit_t, jnp.concatenate(sent, axis=0))
        return carry

    lax.fori_loop(0, blocks, ahead, 0)

    rows = nodes[...]
    pre_node = mm(rows, w_node[...]) + mm(agg[...].astype(BF), w_agg[...]) + node_bias[...]
    node_hidden, node_slope = silu_parts(pre_node)
    node_out = mm(node_hidden.astype(BF), w_node_out[...]) + node_out_bias[...]
    node_unit, node_inverse = norm_parts(node_out)
    new_nodes[...] = (rows.astype(F32) + node_gain[...] * node_unit).astype(BF)
    cot = node_cot[...].astype(F32)
    d_out = norm_back(cot * node_gain[...], node_unit, node_inverse).astype(BF)
    d_hidden = mm_t(d_out, w_node_out[...]).astype(BF).astype(F32)
    d_pre_node = (d_hidden * node_slope).astype(BF)
    d_agg[...] = jnp.zeros(d_agg.shape, BF)
    d_agg[:own] = mm_t(d_pre_node, w_agg[...]).astype(BF)
    d_node[...] = cot + mm_t(d_pre_node, w_node[...])
    sums2[...] = jnp.zeros(sums2.shape, F32)

    def back(index, carry):
        start = pl.multiple_of(index * ROWS, ROWS)
        hit = jnp.concatenate(
            [pick(block_rows(recv, index, part), d_agg.shape[0]) for part in range(parts)], axis=0
        )
        d_sent = mm(hit, d_agg[...])
        outs = []
        for low in range(0, ROWS, CHUNK):
            here = pl.ds(start + low, CHUNK)
            live = jnp.where(index * parts + low // BLOCK < live_count, 1.0, 0.0).astype(F32)
            d_message = edge_cot[here, :].astype(F32) + d_sent[low : low + CHUNK]
            d_unit = d_message * (edge_gain[...] * live)
            outs.append(norm_back(d_unit, unit[here, :], inverse[here, :]).astype(BF))
        d_hid = mm_t(jnp.concatenate(outs, axis=0), w_edge_out[...])
        pres = []
        for low in range(0, ROWS, CHUNK):
            here = pl.ds(start + low, CHUNK)
            part = (d_hid[low : low + CHUNK] * slope[here, :]).astype(BF)
            d_pre[here, :] = part
            pres.append(part)
        hit_t = jnp.concatenate(
            [
                pick_t(
                    remote_index(block_rows(send, index, part), own, near_rows, peers, shift),
                    height,
                )
                for part in range(parts)
            ],
            axis=1,
        )
        sums2[...] += mm(hit_t, jnp.concatenate(pres, axis=0))
        return carry

    lax.fori_loop(0, blocks, back, 0)

    d_rows2 = mm_t(sums2[...].astype(BF), w_send[...])
    for index in range(steps):
        near_out[index][...] = d_rows2[index * near_width : (index + 1) * near_width].astype(BF)
    d_coarse = None
    for slot in range(far_width):
        start = near_rows + slot * peers
        term = mm_l(far_hits[slot], d_rows2[start : start + peers].astype(BF))
        d_coarse = term if d_coarse is None else d_coarse + term
    far_out[...] = d_coarse.astype(BF)


def local_back_kernel(d_pre, edge_cot, d_node, w_edge, w_send, w_recv, send, recv, edge_grad, node_sum, sums):
    own = d_node.shape[0]
    parts = ROWS // LANES
    sums[...] = jnp.zeros(sums.shape, F32)

    def step(index, carry):
        start = pl.multiple_of(index * ROWS, ROWS)
        here = pl.ds(start, ROWS)
        grads = d_pre[here, :]
        value = edge_cot[here, :].astype(F32) + mm_t(grads, w_edge[...])
        edge_grad[here, :] = value.astype(BF)
        hit = jnp.concatenate(
            [
                own_pick_t(
                    send[pl.ds(index * parts + part, 1), :],
                    recv[pl.ds(index * parts + part, 1), :],
                    own,
                )
                for part in range(parts)
            ],
            axis=1,
        )
        sums[...] += mm(hit, grads)
        return carry

    lax.fori_loop(0, d_pre.shape[0] // ROWS, step, 0)
    total = sums[...].astype(BF)
    node_sum[...] = d_node[...] + mm_t(total[:own], w_send[...]) + mm_t(total[own:], w_recv[...])


def combine_kernel(coarse, node_sum, lists, far, *refs):
    steps, width = lists.shape
    near = refs[:steps]
    out, total = refs[steps], refs[steps + 1]
    own = node_sum.shape[0]
    ids = lax.broadcasted_iota(jnp.int32, (own, width), 0)
    value = node_sum[...]
    for index in range(steps):
        value = value + mm(ones_where(ids == lists[index : index + 1, :]), near[index][...])
    total[...] = value
    peers, count, _ = far.shape

    def add(index, carry):
        return carry + far[index].astype(F32)

    grads = lax.fori_loop(0, peers, add, jnp.zeros(far.shape[1:], F32))
    for index in range(count):
        here = pl.ds(coarse[index], 1)
        total[here, :] = total[here, :] + grads[index : index + 1]
    out[...] = total[...].astype(BF)


def vmem(count):
    return [pl.BlockSpec(memory_space=pltpu.VMEM) for _ in range(count)]


def smem():
    return pl.BlockSpec(memory_space=pltpu.SMEM)


def local(
    nodes,
    edges,
    node_cot,
    edge_cot,
    w_edge,
    w_send,
    w_recv,
    edge_bias,
    w_edge_out,
    edge_out_bias,
    edge_gain,
    w_node,
    w_agg,
    node_bias,
    w_node_out,
    node_out_bias,
    node_gain,
    send_slots,
    recv_slots,
    neighbour_send_lists,
    coarse_rows,
    far_lists,
    block_count,
):
    own, width = nodes.shape
    hidden = w_edge.shape[1]
    edge_rows = edges.shape[0]
    peers = lax.axis_size("patch")
    steps, near_width = neighbour_send_lists.shape
    offsets = [(index // 2 + 1) * (1 - 2 * (index % 2)) for index in range(steps)]
    coarse_count = coarse_rows.shape[0]
    far_width = far_lists.shape[2]
    shift = far_width.bit_length() - 1
    if far_width != 1 << shift or own % 64 or edge_rows % ROWS or hidden != width:
        raise ValueError("unsupported sizes")
    slots = steps * near_width + peers * far_width
    height = -(-slots // LANES) * LANES
    own_pad = -(-own // LANES) * LANES
    send = send_slots.reshape(-1, LANES)
    recv = recv_slots.reshape(-1, LANES)
    row = lambda value: value.reshape(1, -1)
    shape = jax.ShapeDtypeStruct

    packed = pl.pallas_call(
        pack_kernel,
        out_shape=[shape((near_width, width), BF)] * steps
        + [shape((peers, coarse_count, width), BF)],
        in_specs=vmem(3),
        out_specs=vmem(steps + 1),
        name="pack",
    )(nodes, neighbour_send_lists, row(coarse_rows))
    near = [passed_along(packed[index], "patch", offsets[index]) for index in range(steps)]
    coarse = lax.all_to_all(
        packed[steps], "patch", split_axis=0, concat_axis=0, tiled=True
    ).reshape(-1, width)

    pre_local = pl.pallas_call(
        local_kernel,
        out_shape=shape((edge_rows, hidden), F32),
        in_specs=vmem(8),
        out_specs=vmem(1)[0],
        scratch_shapes=[pltpu.VMEM((2 * own, hidden), BF)],
        cost_estimate=pl.CostEstimate(
            flops=2 * edge_rows * width * hidden * 3, transcendentals=0, bytes_accessed=6 << 20
        ),
        name="local_ahead",
    )(nodes, edges, w_edge, w_send, w_recv, row(edge_bias), send, recv)

    outs = pl.pallas_call(
        lambda *refs: main_kernel(shift, steps, *refs),
        out_shape=[
            shape((own, width), BF),
            shape((edge_rows, width), BF),
            shape((edge_rows, hidden), BF),
            shape((own, width), F32),
        ]
        + [shape((near_width, width), BF)] * steps
        + [shape((peers * coarse_count, width), BF)],
        in_specs=[smem()] + vmem(19 + steps),
        out_specs=vmem(5 + steps),
        scratch_shapes=[
            pltpu.VMEM((height, width), BF),
            pltpu.VMEM((height, hidden), BF),
            pltpu.VMEM((edge_rows, hidden), F32),
            pltpu.VMEM((edge_rows, width), F32),
            pltpu.VMEM((edge_rows, 1), F32),
            pltpu.VMEM((own, width), F32),
            pltpu.VMEM((own_pad, width), BF),
            pltpu.VMEM((height, hidden), F32),
        ],
        cost_estimate=pl.CostEstimate(
            flops=2 * edge_rows * width * hidden * 8, transcendentals=0, bytes_accessed=16 << 20
        ),
        name="main",
    )(
        block_count,
        pre_local,
        edges,
        edge_cot,
        nodes,
        node_cot,
        send,
        recv,
        far_lists[0],
        coarse,
        *near,
        w_send,
        w_edge_out,
        row(edge_out_bias),
        row(edge_gain),
        w_node,
        w_agg,
        row(node_bias),
        w_node_out,
        row(node_out_bias),
        row(node_gain),
    )
    new_nodes, new_edges, d_pre, d_node = outs[:4]
    returned = [
        passed_along(outs[4 + index], "patch", -offsets[index]) for index in range(steps)
    ]
    far_back = lax.all_to_all(
        outs[4 + steps].reshape(peers, coarse_count, width),
        "patch",
        split_axis=0,
        concat_axis=0,
        tiled=True,
    )

    edge_grad, node_sum = pl.pallas_call(
        local_back_kernel,
        out_shape=[shape((edge_rows, width), BF), shape((own, width), F32)],
        in_specs=vmem(8),
        out_specs=vmem(2),
        scratch_shapes=[pltpu.VMEM((2 * own, hidden), F32)],
        cost_estimate=pl.CostEstimate(
            flops=2 * edge_rows * width * hidden * 3, transcendentals=0, bytes_accessed=6 << 20
        ),
        name="local_back",
    )(d_pre, edge_cot, d_node, w_edge, w_send, w_recv, send, recv)

    node_grad = pl.pallas_call(
        combine_kernel,
        out_shape=shape((own, width), BF),
        in_specs=[smem()] + vmem(3 + steps),
        out_specs=vmem(1)[0],
        scratch_shapes=[pltpu.VMEM((own, width), F32)],
        name="combine",
    )(coarse_rows, node_sum, neighbour_send_lists, far_back, *returned)
    return new_nodes, new_edges, node_grad, edge_grad


def solution(mesh):
    rows = P(("groups", "patch"), None)
    placed = (
        (rows,) * 4
        + (P(),) * 13
        + (
            P("patch"),
            P("patch"),
            P("patch", None),
            P("patch"),
            P("patch", None, None),
            P("patch"),
        )
    )
    return jax.shard_map(
        local,
        mesh=mesh,
        in_specs=placed,
        out_specs=(rows,) * 4,
        check_vma=False,
    )
```

```python
import jax
import jax.numpy as jnp
from jax import lax
from jax.experimental import pallas as pl
from jax.experimental.pallas import tpu as pltpu
from jax.sharding import PartitionSpec as P

BLOCK = 128
LANES = 128
ROWS = 256
CHUNK = 32
FIXED = 7
EPS = 1e-05
BF = jnp.bfloat16
F32 = jnp.float32


def passed_along(value, axis, steps):
    count = lax.axis_size(axis)
    pairs = [(source, (source + steps) % count) for source in range(count)]
    return lax.ppermute(value, axis, pairs)


def mm(a, b):
    return lax.dot_general(a, b, (((1,), (0,)), ((), ())), preferred_element_type=F32)


def mm_t(a, b):
    return lax.dot_general(a, b, (((1,), (1,)), ((), ())), preferred_element_type=F32)


def mm_l(a, b):
    return lax.dot_general(a, b, (((0,), (0,)), ((), ())), preferred_element_type=F32)


def ones_where(mask):
    return jnp.where(mask, 1.0, 0.0).astype(BF)


def as_columns(row):
    return jnp.broadcast_to(row.astype(F32), (LANES, LANES)).T.astype(jnp.int32)


def lane_ids(tile):
    return lax.broadcasted_iota(jnp.int32, (LANES, LANES), 1) + tile * LANES


def own_pick(send, recv, own):
    sender = as_columns(jnp.where(send < own, send, -1))
    receiver = as_columns(recv + own)
    tiles = []
    for tile in range(2 * own // LANES):
        ids = lane_ids(tile)
        if (tile + 1) * LANES <= own:
            hit = sender == ids
        elif tile * LANES >= own:
            hit = receiver == ids
        else:
            hit = (sender == ids) | (receiver == ids)
        tiles.append(ones_where(hit))
    return jnp.concatenate(tiles, axis=1)


def own_pick_t(send, recv, own):
    sender = jnp.where(send < own, send, -1)
    ids = lax.broadcasted_iota(jnp.int32, (own, LANES), 0)
    return jnp.concatenate([ones_where(ids == sender), ones_where(ids == recv)], axis=0)


def remote_index(send, own, near, peers, shift):
    far = send - (own + near)
    far_index = near + (far & ((1 << shift) - 1)) * peers + (far >> shift)
    return jnp.where(send < own + near, send - own, far_index)


def pick(row, width):
    column = as_columns(row)
    return jnp.concatenate(
        [ones_where(column == lane_ids(tile)) for tile in range(width // LANES)], axis=1
    )


def pick_t(row, height):
    return ones_where(lax.broadcasted_iota(jnp.int32, (height, LANES), 0) == row)


def silu_parts(value):
    gate = 0.5 * jnp.tanh(0.5 * value) + 0.5
    hidden = value * gate
    slope = gate * (1.0 + value - hidden)
    return hidden, slope


def norm_parts(value):
    center = value - jnp.mean(value, axis=-1, keepdims=True)
    inverse = lax.rsqrt(jnp.mean(center * center, axis=-1, keepdims=True) + EPS)
    return center * inverse, inverse


def norm_back(grad, unit, inverse):
    first = jnp.mean(grad, axis=-1, keepdims=True)
    second = jnp.mean(grad * unit, axis=-1, keepdims=True)
    return inverse * (grad - first - unit * second)


def pack_kernel(nodes, lists, coarse, *outs):
    rows = nodes[...]
    own = rows.shape[0]
    steps, width = lists.shape
    ids = lax.broadcasted_iota(jnp.int32, (own, width), 0)
    for index in range(steps):
        hit = ones_where(ids == lists[index : index + 1, :])
        outs[index][...] = mm_l(hit, rows).astype(BF)
    count = coarse.shape[1]
    hit = ones_where(lax.broadcasted_iota(jnp.int32, (own, count), 0) == coarse[...])
    picked = mm_l(hit, rows).astype(BF)
    out = outs[steps]

    def put(index, carry):
        out[index] = picked
        return carry

    lax.fori_loop(0, out.shape[0], put, 0)


def local_kernel(bias, send, recv, nodes_in, edges_in, w_send_in, w_recv_in, w_edge_in, out, *scratch):
    nodes, edges, w_send, w_recv, w_edge, table, value, load, store = scratch
    own = nodes.shape[0]
    parts = ROWS // LANES
    blocks = edges.shape[0] // ROWS
    fixed = [
        pltpu.make_async_copy(source, target, load.at[index])
        for index, (source, target) in enumerate(
            [(nodes_in, nodes), (w_send_in, w_send), (w_recv_in, w_recv), (w_edge_in, w_edge)]
        )
    ]

    def block_in(index):
        here = pl.ds(pl.multiple_of(index * ROWS, ROWS), ROWS)
        return pltpu.make_async_copy(edges_in.at[here, :], edges.at[here, :], load.at[4 + index])

    def block_out(index):
        here = pl.ds(pl.multiple_of(index * ROWS, ROWS), ROWS)
        return pltpu.make_async_copy(value.at[here, :], out.at[here, :], store.at[index])

    for copy in fixed:
        copy.start()
    for index in range(blocks):
        block_in(index).start()
    fixed[0].wait()
    fixed[1].wait()
    rows = nodes[...]
    table[:own] = mm(rows, w_send[...]).astype(BF)
    fixed[2].wait()
    table[own:] = mm(rows, w_recv[...]).astype(BF)
    fixed[3].wait()

    def step(index, carry):
        here = pl.ds(pl.multiple_of(index * ROWS, ROWS), ROWS)
        hit = jnp.concatenate(
            [
                own_pick(
                    send[pl.ds(index * parts + part, 1), :],
                    recv[pl.ds(index * parts + part, 1), :],
                    own,
                )
                for part in range(parts)
            ],
            axis=0,
        )
        near = mm(hit, table[...]) + bias[...]
        block_in(index).wait()
        value[here, :] = near + mm(edges[here, :], w_edge[...])
        block_out(index).start()
        return carry

    lax.fori_loop(0, blocks, step, 0)
    for index in range(blocks):
        block_out(index).wait()


def main_kernel(shift, steps, *refs):
    take = iter(refs)
    count, send, recv, far_lists = [next(take) for _ in range(4)]
    edge_out_bias, edge_gain, node_bias, node_out_bias, node_gain = [next(take) for _ in range(5)]
    near = [next(take) for _ in range(steps)]
    coarse = next(take)
    sources = [next(take) for _ in range(FIXED + 3)]
    new_nodes, new_edges_out, d_pre_out, d_node = [next(take) for _ in range(4)]
    near_out = [next(take) for _ in range(steps)]
    far_out = next(take)
    targets = [next(take) for _ in range(FIXED + 3)]
    new_edges, d_pre = [next(take) for _ in range(2)]
    rows2, table2, slope, unit, inverse, agg, d_agg, sums2 = [next(take) for _ in range(8)]
    load, store = next(take), next(take)
    w_send, w_edge_out, nodes, w_agg, w_node, w_node_out, node_cot = targets[:FIXED]
    pre_in, edges, edge_cot = targets[FIXED:]
    own = nodes.shape[0]
    width = nodes.shape[1]
    peers, far_width = far_lists.shape
    near_width = near[0].shape[0]
    near_rows = steps * near_width
    height = table2.shape[0]
    coarse_rows = coarse.shape[0] // peers
    parts = ROWS // LANES
    blocks = edges.shape[0] // ROWS
    live_count = count[0]
    fixed = [
        pltpu.make_async_copy(sources[index], targets[index], load.at[index])
        for index in range(FIXED)
    ]

    def block_in(which, index):
        here = pl.ds(pl.multiple_of(index * ROWS, ROWS), ROWS)
        return pltpu.make_async_copy(
            sources[FIXED + which].at[here, :],
            targets[FIXED + which].at[here, :],
            load.at[FIXED + which * blocks + index],
        )

    def block_out(which, index):
        here = pl.ds(pl.multiple_of(index * ROWS, ROWS), ROWS)
        source, target = ((new_edges, new_edges_out), (d_pre, d_pre_out))[which]
        return pltpu.make_async_copy(
            source.at[here, :], target.at[here, :], store.at[which * blocks + index]
        )

    fixed[0].start()
    block_in(0, 0).start()
    block_in(1, 0).start()
    fixed[1].start()
    for index in range(1, blocks):
        block_in(0, index).start()
        block_in(1, index).start()
    for copy in fixed[2:]:
        copy.start()
    for index in range(blocks):
        block_in(2, index).start()

    far_ids = lax.broadcasted_iota(jnp.int32, (peers, coarse.shape[0]), 1)
    far_base = lax.broadcasted_iota(jnp.int32, (peers, coarse.shape[0]), 0) * coarse_rows
    far_hits = [
        ones_where(far_ids == far_base + far_lists[:, slot : slot + 1])
        for slot in range(far_width)
    ]
    rows2[...] = jnp.zeros(rows2.shape, BF)
    for index in range(steps):
        rows2[index * near_width : (index + 1) * near_width] = near[index][...]
    for slot in range(far_width):
        start = near_rows + slot * peers
        rows2[start : start + peers] = mm(far_hits[slot], coarse[...]).astype(BF)
    fixed[0].wait()
    table2[...] = mm(rows2[...], w_send[...]).astype(BF)
    fixed[1].wait()
    agg[...] = jnp.zeros(agg.shape, F32)

    def block_rows(ref, index, part):
        return ref[pl.ds(index * parts + part, 1), :]

    def ahead(index, carry):
        start = pl.multiple_of(index * ROWS, ROWS)
        hit = jnp.concatenate(
            [
                pick(remote_index(block_rows(send, index, part), own, near_rows, peers, shift), height)
                for part in range(parts)
            ],
            axis=0,
        )
        remote = mm(hit, table2[...])
        block_in(0, index).wait()
        block_in(1, index).wait()
        hidden = []
        for low in range(0, ROWS, CHUNK):
            here = pl.ds(start + low, CHUNK)
            value = pre_in[here, :] + remote[low : low + CHUNK]
            part_hidden, part_slope = silu_parts(value)
            slope[here, :] = part_slope
            hidden.append(part_hidden.astype(BF))
        out = mm(jnp.concatenate(hidden, axis=0), w_edge_out[...])
        sent = []
        for low in range(0, ROWS, CHUNK):
            here = pl.ds(start + low, CHUNK)
            live = jnp.where(index * parts + low // BLOCK < live_count, 1.0, 0.0).astype(F32)
            part_unit, part_inverse = norm_parts(out[low : low + CHUNK] + edge_out_bias[...])
            unit[here, :] = part_unit
            inverse[here, :] = part_inverse
            message = part_unit * (edge_gain[...] * live)
            new_edges[here, :] = (edges[here, :].astype(F32) + message).astype(BF)
            sent.append(message.astype(BF))
        block_out(0, index).start()
        hit_t = jnp.concatenate(
            [pick_t(block_rows(recv, index, part), own) for part in range(parts)], axis=1
        )
        agg[...] += mm(hit_t, jnp.concatenate(sent, axis=0))
        return carry

    lax.fori_loop(0, blocks, ahead, 0)

    for copy in fixed[2:]:
        copy.wait()
    rows = nodes[...]
    pre_node = mm(rows, w_node[...]) + mm(agg[...].astype(BF), w_agg[...]) + node_bias[...]
    node_hidden, node_slope = silu_parts(pre_node)
    node_out = mm(node_hidden.astype(BF), w_node_out[...]) + node_out_bias[...]
    node_unit, node_inverse = norm_parts(node_out)
    new_nodes[...] = (rows.astype(F32) + node_gain[...] * node_unit).astype(BF)
    cot = node_cot[...].astype(F32)
    d_out = norm_back(cot * node_gain[...], node_unit, node_inverse).astype(BF)
    d_hidden = mm_t(d_out, w_node_out[...]).astype(BF).astype(F32)
    d_pre_node = (d_hidden * node_slope).astype(BF)
    d_agg[...] = jnp.zeros(d_agg.shape, BF)
    d_agg[:own] = mm_t(d_pre_node, w_agg[...]).astype(BF)
    d_node[...] = cot + mm_t(d_pre_node, w_node[...])
    sums2[...] = jnp.zeros(sums2.shape, F32)

    def back(index, carry):
        start = pl.multiple_of(index * ROWS, ROWS)
        hit = jnp.concatenate(
            [pick(block_rows(recv, index, part), d_agg.shape[0]) for part in range(parts)], axis=0
        )
        d_sent = mm(hit, d_agg[...])
        block_in(2, index).wait()
        outs = []
        for low in range(0, ROWS, CHUNK):
            here = pl.ds(start + low, CHUNK)
            live = jnp.where(index * parts + low // BLOCK < live_count, 1.0, 0.0).astype(F32)
            d_message = edge_cot[here, :].astype(F32) + d_sent[low : low + CHUNK]
            d_unit = d_message * (edge_gain[...] * live)
            outs.append(norm_back(d_unit, unit[here, :], inverse[here, :]).astype(BF))
        d_hid = mm_t(jnp.concatenate(outs, axis=0), w_edge_out[...])
        pres = []
        for low in range(0, ROWS, CHUNK):
            here = pl.ds(start + low, CHUNK)
            part = (d_hid[low : low + CHUNK] * slope[here, :]).astype(BF)
            d_pre[here, :] = part
            pres.append(part)
        block_out(1, index).start()
        hit_t = jnp.concatenate(
            [
                pick_t(
                    remote_index(block_rows(send, index, part), own, near_rows, peers, shift),
                    height,
                )
                for part in range(parts)
            ],
            axis=1,
        )
        sums2[...] += mm(hit_t, jnp.concatenate(pres, axis=0))
        return carry

    lax.fori_loop(0, blocks, back, 0)

    d_rows2 = mm_t(sums2[...].astype(BF), w_send[...])
    for index in range(steps):
        near_out[index][...] = d_rows2[index * near_width : (index + 1) * near_width].astype(BF)
    d_coarse = None
    for slot in range(far_width):
        start = near_rows + slot * peers
        term = mm_l(far_hits[slot], d_rows2[start : start + peers].astype(BF))
        d_coarse = term if d_coarse is None else d_coarse + term
    far_out[...] = d_coarse.astype(BF)
    for index in range(blocks):
        block_out(0, index).wait()
        block_out(1, index).wait()


def local_back_kernel(send, recv, d_pre_in, cot_in, w_edge_in, w_send_in, w_recv_in, d_node_in, *refs):
    edge_grad_out, node_sum = refs[:2]
    d_pre, cot, w_edge, w_send, w_recv, d_node, edge_grad, sums, load, store = refs[2:]
    own = d_node.shape[0]
    parts = ROWS // LANES
    blocks = d_pre.shape[0] // ROWS
    fixed = [
        pltpu.make_async_copy(source, target, load.at[index])
        for index, (source, target) in enumerate(
            [(w_edge_in, w_edge), (w_send_in, w_send), (w_recv_in, w_recv), (d_node_in, d_node)]
        )
    ]

    def block_in(which, index):
        here = pl.ds(pl.multiple_of(index * ROWS, ROWS), ROWS)
        source, target = ((d_pre_in, d_pre), (cot_in, cot))[which]
        return pltpu.make_async_copy(
            source.at[here, :], target.at[here, :], load.at[4 + which * blocks + index]
        )

    def block_out(index):
        here = pl.ds(pl.multiple_of(index * ROWS, ROWS), ROWS)
        return pltpu.make_async_copy(edge_grad.at[here, :], edge_grad_out.at[here, :], store.at[index])

    fixed[0].start()
    for index in range(blocks):
        block_in(0, index).start()
        block_in(1, index).start()
    for copy in fixed[1:]:
        copy.start()
    sums[...] = jnp.zeros(sums.shape, F32)
    fixed[0].wait()

    def step(index, carry):
        here = pl.ds(pl.multiple_of(index * ROWS, ROWS), ROWS)
        hit = jnp.concatenate(
            [
                own_pick_t(
                    send[pl.ds(index * parts + part, 1), :],
                    recv[pl.ds(index * parts + part, 1), :],
                    own,
                )
                for part in range(parts)
            ],
            axis=1,
        )
        block_in(0, index).wait()
        block_in(1, index).wait()
        grads = d_pre[here, :]
        value = cot[here, :].astype(F32) + mm_t(grads, w_edge[...])
        edge_grad[here, :] = value.astype(BF)
        block_out(index).start()
        sums[...] += mm(hit, grads)
        return carry

    lax.fori_loop(0, blocks, step, 0)
    for copy in fixed[1:]:
        copy.wait()
    total = sums[...].astype(BF)
    node_sum[...] = d_node[...] + mm_t(total[:own], w_send[...]) + mm_t(total[own:], w_recv[...])
    for index in range(blocks):
        block_out(index).wait()


def combine_kernel(coarse, node_sum, lists, far, *refs):
    steps, width = lists.shape
    near = refs[:steps]
    out, total = refs[steps], refs[steps + 1]
    own = node_sum.shape[0]
    ids = lax.broadcasted_iota(jnp.int32, (own, width), 0)
    value = node_sum[...]
    for index in range(steps):
        value = value + mm(ones_where(ids == lists[index : index + 1, :]), near[index][...])
    total[...] = value
    peers, count, _ = far.shape

    def add(index, carry):
        return carry + far[index].astype(F32)

    grads = lax.fori_loop(0, peers, add, jnp.zeros(far.shape[1:], F32))
    for index in range(count):
        here = pl.ds(coarse[index], 1)
        total[here, :] = total[here, :] + grads[index : index + 1]
    out[...] = total[...].astype(BF)


def vmem(count):
    return [pl.BlockSpec(memory_space=pltpu.VMEM) for _ in range(count)]


def hbm(count):
    return [pl.BlockSpec(memory_space=pltpu.HBM) for _ in range(count)]


def smem():
    return pl.BlockSpec(memory_space=pltpu.SMEM)


def local(
    nodes,
    edges,
    node_cot,
    edge_cot,
    w_edge,
    w_send,
    w_recv,
    edge_bias,
    w_edge_out,
    edge_out_bias,
    edge_gain,
    w_node,
    w_agg,
    node_bias,
    w_node_out,
    node_out_bias,
    node_gain,
    send_slots,
    recv_slots,
    neighbour_send_lists,
    coarse_rows,
    far_lists,
    block_count,
):
    own, width = nodes.shape
    hidden = w_edge.shape[1]
    edge_rows = edges.shape[0]
    peers = lax.axis_size("patch")
    steps, near_width = neighbour_send_lists.shape
    offsets = [(index // 2 + 1) * (1 - 2 * (index % 2)) for index in range(steps)]
    coarse_count = coarse_rows.shape[0]
    far_width = far_lists.shape[2]
    shift = far_width.bit_length() - 1
    if far_width != 1 << shift or own % 64 or edge_rows % ROWS or hidden != width:
        raise ValueError("unsupported sizes")
    slots = steps * near_width + peers * far_width
    height = -(-slots // LANES) * LANES
    own_pad = -(-own // LANES) * LANES
    send = send_slots.reshape(-1, LANES)
    recv = recv_slots.reshape(-1, LANES)
    blocks = edge_rows // ROWS
    row = lambda value: value.reshape(1, -1)
    shape = jax.ShapeDtypeStruct

    packed = pl.pallas_call(
        pack_kernel,
        out_shape=[shape((near_width, width), BF)] * steps
        + [shape((peers, coarse_count, width), BF)],
        in_specs=vmem(3),
        out_specs=vmem(steps + 1),
        name="pack",
    )(nodes, neighbour_send_lists, row(coarse_rows))
    near = [passed_along(packed[index], "patch", offsets[index]) for index in range(steps)]
    coarse = lax.all_to_all(
        packed[steps], "patch", split_axis=0, concat_axis=0, tiled=True
    ).reshape(-1, width)

    pre_local = pl.pallas_call(
        local_kernel,
        out_shape=shape((edge_rows, hidden), F32),
        in_specs=vmem(3) + hbm(5),
        out_specs=hbm(1)[0],
        scratch_shapes=[
            pltpu.VMEM((own, width), BF),
            pltpu.VMEM((edge_rows, width), BF),
            pltpu.VMEM((width, hidden), BF),
            pltpu.VMEM((width, hidden), BF),
            pltpu.VMEM((width, hidden), BF),
            pltpu.VMEM((2 * own, hidden), BF),
            pltpu.VMEM((edge_rows, hidden), F32),
            pltpu.SemaphoreType.DMA((4 + blocks,)),
            pltpu.SemaphoreType.DMA((blocks,)),
        ],
        cost_estimate=pl.CostEstimate(
            flops=2 * edge_rows * width * hidden * 3, transcendentals=0, bytes_accessed=6 << 20
        ),
        name="local_ahead",
    )(row(edge_bias), send, recv, nodes, edges, w_send, w_recv, w_edge)

    outs = pl.pallas_call(
        lambda *refs: main_kernel(shift, steps, *refs),
        out_shape=[
            shape((own, width), BF),
            shape((edge_rows, width), BF),
            shape((edge_rows, hidden), BF),
            shape((own, width), F32),
        ]
        + [shape((near_width, width), BF)] * steps
        + [shape((peers * coarse_count, width), BF)],
        in_specs=[smem()] + vmem(9 + steps) + hbm(FIXED + 3),
        out_specs=vmem(1) + hbm(2) + vmem(2 + steps),
        scratch_shapes=[
            pltpu.VMEM((width, hidden), BF),
            pltpu.VMEM((hidden, width), BF),
            pltpu.VMEM((own, width), BF),
            pltpu.VMEM((width, hidden), BF),
            pltpu.VMEM((width, hidden), BF),
            pltpu.VMEM((hidden, width), BF),
            pltpu.VMEM((own, width), BF),
            pltpu.VMEM((edge_rows, hidden), F32),
            pltpu.VMEM((edge_rows, width), BF),
            pltpu.VMEM((edge_rows, width), BF),
            pltpu.VMEM((edge_rows, width), BF),
            pltpu.VMEM((edge_rows, hidden), BF),
            pltpu.VMEM((height, width), BF),
            pltpu.VMEM((height, hidden), BF),
            pltpu.VMEM((edge_rows, hidden), F32),
            pltpu.VMEM((edge_rows, width), F32),
            pltpu.VMEM((edge_rows, 1), F32),
            pltpu.VMEM((own, width), F32),
            pltpu.VMEM((own_pad, width), BF),
            pltpu.VMEM((height, hidden), F32),
            pltpu.SemaphoreType.DMA((FIXED + 3 * blocks,)),
            pltpu.SemaphoreType.DMA((2 * blocks,)),
        ],
        cost_estimate=pl.CostEstimate(
            flops=2 * edge_rows * width * hidden * 8, transcendentals=0, bytes_accessed=16 << 20
        ),
        name="main",
    )(
        block_count,
        send,
        recv,
        far_lists[0],
        row(edge_out_bias),
        row(edge_gain),
        row(node_bias),
        row(node_out_bias),
        row(node_gain),
        *near,
        coarse,
        w_send,
        w_edge_out,
        nodes,
        w_agg,
        w_node,
        w_node_out,
        node_cot,
        pre_local,
        edges,
        edge_cot,
    )
    new_nodes, new_edges, d_pre, d_node = outs[:4]
    returned = [
        passed_along(outs[4 + index], "patch", -offsets[index]) for index in range(steps)
    ]
    far_back = lax.all_to_all(
        outs[4 + steps].reshape(peers, coarse_count, width),
        "patch",
        split_axis=0,
        concat_axis=0,
        tiled=True,
    )

    edge_grad, node_sum = pl.pallas_call(
        local_back_kernel,
        out_shape=[shape((edge_rows, width), BF), shape((own, width), F32)],
        in_specs=vmem(2) + hbm(6),
        out_specs=hbm(1) + vmem(1),
        scratch_shapes=[
            pltpu.VMEM((edge_rows, hidden), BF),
            pltpu.VMEM((edge_rows, width), BF),
            pltpu.VMEM((width, hidden), BF),
            pltpu.VMEM((width, hidden), BF),
            pltpu.VMEM((width, hidden), BF),
            pltpu.VMEM((own, width), F32),
            pltpu.VMEM((edge_rows, width), BF),
            pltpu.VMEM((2 * own, hidden), F32),
            pltpu.SemaphoreType.DMA((4 + 2 * blocks,)),
            pltpu.SemaphoreType.DMA((blocks,)),
        ],
        cost_estimate=pl.CostEstimate(
            flops=2 * edge_rows * width * hidden * 3, transcendentals=0, bytes_accessed=6 << 20
        ),
        name="local_back",
    )(send, recv, d_pre, edge_cot, w_edge, w_send, w_recv, d_node)

    node_grad = pl.pallas_call(
        combine_kernel,
        out_shape=shape((own, width), BF),
        in_specs=[smem()] + vmem(3 + steps),
        out_specs=vmem(1)[0],
        scratch_shapes=[pltpu.VMEM((own, width), F32)],
        name="combine",
    )(coarse_rows, node_sum, neighbour_send_lists, far_back, *returned)
    return new_nodes, new_edges, node_grad, edge_grad


def solution(mesh):
    rows = P(("groups", "patch"), None)
    placed = (
        (rows,) * 4
        + (P(),) * 13
        + (
            P("patch"),
            P("patch"),
            P("patch", None),
            P("patch"),
            P("patch", None, None),
            P("patch"),
        )
    )
    return jax.shard_map(
        local,
        mesh=mesh,
        in_specs=placed,
        out_specs=(rows,) * 4,
        check_vma=False,
    )
```

```python
import jax
import jax.numpy as jnp
from jax import lax
from jax.experimental import pallas as pl
from jax.experimental.pallas import tpu as pltpu
from jax.sharding import PartitionSpec as P

BLOCK = 128
LANES = 128
ROWS = 512
MAIN_ROWS = 1536
COPY = 256
CHUNK = 16
FIXED = 15
EPS = 1e-05
BF = jnp.bfloat16
F32 = jnp.float32


def passed_along(value, axis, steps):
    count = lax.axis_size(axis)
    pairs = [(source, (source + steps) % count) for source in range(count)]
    return lax.ppermute(value, axis, pairs)


def mm(a, b):
    return lax.dot_general(a, b, (((1,), (0,)), ((), ())), preferred_element_type=F32)


def mm_t(a, b):
    return lax.dot_general(a, b, (((1,), (1,)), ((), ())), preferred_element_type=F32)


def mm_l(a, b):
    return lax.dot_general(a, b, (((0,), (0,)), ((), ())), preferred_element_type=F32)


def ones_where(mask):
    return jnp.where(mask, 1.0, 0.0).astype(BF)


def as_columns(row):
    return jnp.broadcast_to(row.astype(F32), (LANES, LANES)).T.astype(jnp.int32)


def lane_ids(tile):
    return lax.broadcasted_iota(jnp.int32, (LANES, LANES), 1) + tile * LANES


def own_pick(send, recv, own):
    sender = as_columns(jnp.where(send < own, send, -1))
    receiver = as_columns(recv + own)
    tiles = []
    for tile in range(2 * own // LANES):
        ids = lane_ids(tile)
        if (tile + 1) * LANES <= own:
            hit = sender == ids
        elif tile * LANES >= own:
            hit = receiver == ids
        else:
            hit = (sender == ids) | (receiver == ids)
        tiles.append(ones_where(hit))
    return jnp.concatenate(tiles, axis=1)


def own_pick_t(send, recv, own):
    sender = jnp.where(send < own, send, -1)
    ids = lax.broadcasted_iota(jnp.int32, (own, LANES), 0)
    return jnp.concatenate([ones_where(ids == sender), ones_where(ids == recv)], axis=0)


def remote_index(send, own, near, peers, shift):
    far = send - (own + near)
    far_index = near + (far & ((1 << shift) - 1)) * peers + (far >> shift)
    return jnp.where(send < own + near, send - own, far_index)


def pick(row, width):
    column = as_columns(row)
    return jnp.concatenate(
        [ones_where(column == lane_ids(tile)) for tile in range(width // LANES)], axis=1
    )


def pick_t(row, height):
    return ones_where(lax.broadcasted_iota(jnp.int32, (height, LANES), 0) == row)


def silu_parts(value):
    gate = 0.5 * jnp.tanh(0.5 * value) + 0.5
    hidden = value * gate
    slope = gate * (1.0 + value - hidden)
    return hidden, slope


def norm_parts(value):
    center = value - jnp.mean(value, axis=-1, keepdims=True)
    inverse = lax.rsqrt(jnp.mean(center * center, axis=-1, keepdims=True) + EPS)
    return center * inverse, inverse


def norm_back(grad, unit, inverse):
    first = jnp.mean(grad, axis=-1, keepdims=True)
    second = jnp.mean(grad * unit, axis=-1, keepdims=True)
    return inverse * (grad - first - unit * second)


def copies_of(sources, targets, sems):
    return [
        pltpu.make_async_copy(source, target, sems.at[index])
        for index, (source, target) in enumerate(zip(sources, targets))
    ]


def start_all(copies):
    for copy in copies:
        copy.start()


def wait_all(copies):
    for copy in copies:
        copy.wait()


def rows_of(index):
    return pl.ds(pl.multiple_of(index * COPY, COPY), COPY)


def pack_kernel(nodes, lists, coarse, *outs):
    rows = nodes[...]
    own = rows.shape[0]
    steps, width = lists.shape
    ids = lax.broadcasted_iota(jnp.int32, (own, width), 0)
    for index in range(steps):
        hit = ones_where(ids == lists[index : index + 1, :])
        outs[index][...] = mm_l(hit, rows).astype(BF)
    count = coarse.shape[1]
    hit = ones_where(lax.broadcasted_iota(jnp.int32, (own, count), 0) == coarse[...])
    picked = mm_l(hit, rows).astype(BF)
    out = outs[steps]

    def put(index, carry):
        out[index] = picked
        return carry

    lax.fori_loop(0, out.shape[0], put, 0)


def local_kernel(*refs):
    sources, edges_in, out = refs[:7], refs[7], refs[8]
    targets, edges, table, value, load, store = refs[9:16], *refs[16:]
    nodes, w_send, w_recv, send, recv, w_edge, bias = targets
    own = nodes.shape[0]
    parts = ROWS // LANES
    copies = edges.shape[0] // COPY
    ratio = ROWS // COPY
    fixed = copies_of(sources, targets, load)

    def block_in(index):
        here = rows_of(index)
        return pltpu.make_async_copy(edges_in.at[here, :], edges.at[here, :], load.at[7 + index])

    def block_out(index):
        here = rows_of(index)
        return pltpu.make_async_copy(value.at[here, :], out.at[here, :], store.at[index])

    start_all(fixed)
    for index in range(copies):
        block_in(index).start()
    wait_all(fixed[:2])
    rows = nodes[...]
    table[:own] = mm(rows, w_send[...]).astype(BF)
    fixed[2].wait()
    table[own:] = mm(rows, w_recv[...]).astype(BF)
    wait_all(fixed[3:])

    def step(index, carry):
        here = pl.ds(pl.multiple_of(index * ROWS, ROWS), ROWS)
        hit = jnp.concatenate(
            [
                own_pick(
                    send[pl.ds(index * parts + part, 1), :],
                    recv[pl.ds(index * parts + part, 1), :],
                    own,
                )
                for part in range(parts)
            ],
            axis=0,
        )
        near = mm(hit, table[...]) + bias[...]
        for part in range(ratio):
            block_in(index * ratio + part).wait()
        value[here, :] = (near + mm(edges[here, :], w_edge[...])).astype(BF)
        for part in range(ratio):
            block_out(index * ratio + part).start()
        return carry

    lax.fori_loop(0, edges.shape[0] // ROWS, step, 0)
    for index in range(copies):
        block_out(index).wait()


def main_kernel(shift, steps, *refs):
    take = iter(refs)
    count = next(take)
    near = [next(take) for _ in range(steps)]
    coarse = next(take)
    sources = [next(take) for _ in range(FIXED)]
    block_sources = [next(take) for _ in range(3)]
    near_out = [next(take) for _ in range(steps)]
    far_out = next(take)
    new_nodes_out, d_node_out, new_edges_out, d_pre_out = [next(take) for _ in range(4)]
    targets = [next(take) for _ in range(FIXED)]
    pre_in, edges, edge_cot = block_targets = [next(take) for _ in range(3)]
    new_nodes, d_node, new_edges, d_pre = [next(take) for _ in range(4)]
    rows2, table2, slope, unit, inverse, agg, d_agg, sums2 = [next(take) for _ in range(8)]
    load, store = next(take), next(take)
    far_lists, w_send, send, recv, w_edge_out, edge_out_bias, edge_gain = targets[:7]
    nodes, w_agg, w_node, node_bias, w_node_out, node_out_bias, node_cot, node_gain = targets[7:]
    own = nodes.shape[0]
    width = nodes.shape[1]
    far_width, peers = far_lists.shape
    near_width = near[0].shape[0]
    near_rows = steps * near_width
    height = table2.shape[0]
    coarse_rows = coarse.shape[0] // peers
    parts = MAIN_ROWS // LANES
    blocks = edges.shape[0] // MAIN_ROWS
    copies = edges.shape[0] // COPY
    ratio = MAIN_ROWS // COPY
    live_count = count[0]
    fixed = copies_of(sources, targets, load)

    def block_in(which, index):
        here = rows_of(index)
        return pltpu.make_async_copy(
            block_sources[which].at[here, :],
            block_targets[which].at[here, :],
            load.at[FIXED + which * copies + index],
        )

    def block_out(which, index):
        here = rows_of(index)
        source, target = ((new_edges, new_edges_out), (d_pre, d_pre_out))[which]
        return pltpu.make_async_copy(
            source.at[here, :], target.at[here, :], store.at[which * copies + index]
        )

    node_outs = [
        pltpu.make_async_copy(new_nodes, new_nodes_out, store.at[2 * copies]),
        pltpu.make_async_copy(d_node, d_node_out, store.at[2 * copies + 1]),
    ]
    start_all(fixed[:4])
    block_in(0, 0).start()
    start_all(fixed[4:7])
    block_in(1, 0).start()
    for index in range(1, copies):
        block_in(0, index).start()
        block_in(1, index).start()
    start_all(fixed[7:])
    for index in range(copies):
        block_in(2, index).start()

    fixed[0].wait()
    far_ids = lax.broadcasted_iota(jnp.int32, (coarse.shape[0], peers), 0)
    far_base = lax.broadcasted_iota(jnp.int32, (coarse.shape[0], peers), 1) * coarse_rows
    far_hits = [
        ones_where(far_ids == far_base + far_lists[slot : slot + 1, :])
        for slot in range(far_width)
    ]
    rows2[...] = jnp.zeros(rows2.shape, BF)
    for index in range(steps):
        rows2[index * near_width : (index + 1) * near_width] = near[index][...]
    for slot in range(far_width):
        start = near_rows + slot * peers
        rows2[start : start + peers] = mm_l(far_hits[slot], coarse[...]).astype(BF)
    fixed[1].wait()
    table2[...] = mm(rows2[...], w_send[...]).astype(BF)
    wait_all(fixed[2:4])
    agg[...] = jnp.zeros(agg.shape, F32)
    wait_all(fixed[4:7])

    def block_rows(ref, index, part):
        return ref[pl.ds(index * parts + part, 1), :]

    def ahead(index, carry):
        start = pl.multiple_of(index * MAIN_ROWS, MAIN_ROWS)
        hit = jnp.concatenate(
            [
                pick(remote_index(block_rows(send, index, part), own, near_rows, peers, shift), height)
                for part in range(parts)
            ],
            axis=0,
        )
        remote = mm(hit, table2[...])
        hidden = []
        for low in range(0, MAIN_ROWS, CHUNK):
            if low % COPY == 0:
                block_in(0, index * ratio + low // COPY).wait()
            here = pl.ds(start + low, CHUNK)
            value = pre_in[here, :].astype(F32) + remote[low : low + CHUNK]
            part_hidden, part_slope = silu_parts(value)
            slope[here, :] = part_slope
            hidden.append(part_hidden.astype(BF))
        out = mm(jnp.concatenate(hidden, axis=0), w_edge_out[...])
        sent = []
        for low in range(0, MAIN_ROWS, CHUNK):
            if low % COPY == 0:
                block_in(1, index * ratio + low // COPY).wait()
            here = pl.ds(start + low, CHUNK)
            if low % BLOCK == 0:
                live = jnp.where(index * parts + low // BLOCK < live_count, 1.0, 0.0)
                live_gain = edge_gain[...] * live.astype(F32)
            part_unit, part_inverse = norm_parts(out[low : low + CHUNK] + edge_out_bias[...])
            unit[here, :] = part_unit
            inverse[here, :] = part_inverse
            message = part_unit * live_gain
            new_edges[here, :] = (edges[here, :].astype(F32) + message).astype(BF)
            sent.append(message.astype(BF))
            if (low + CHUNK) % COPY == 0:
                block_out(0, index * ratio + low // COPY).start()
        hit_t = jnp.concatenate(
            [pick_t(block_rows(recv, index, part), own) for part in range(parts)], axis=1
        )
        agg[...] += mm(hit_t, jnp.concatenate(sent, axis=0))
        return carry

    lax.fori_loop(0, blocks, ahead, 0)

    wait_all(fixed[7:])
    rows = nodes[...]
    pre_node = mm(rows, w_node[...]) + mm(agg[...].astype(BF), w_agg[...]) + node_bias[...]
    node_hidden, node_slope = silu_parts(pre_node)
    node_out = mm(node_hidden.astype(BF), w_node_out[...]) + node_out_bias[...]
    node_unit, node_inverse = norm_parts(node_out)
    new_nodes[...] = (rows.astype(F32) + node_gain[...] * node_unit).astype(BF)
    cot = node_cot[...].astype(F32)
    d_out = norm_back(cot * node_gain[...], node_unit, node_inverse).astype(BF)
    d_hidden = mm_t(d_out, w_node_out[...]).astype(BF).astype(F32)
    d_pre_node = (d_hidden * node_slope).astype(BF)
    d_agg[...] = jnp.zeros(d_agg.shape, BF)
    d_agg[:own] = mm_t(d_pre_node, w_agg[...]).astype(BF)
    d_node[...] = cot + mm_t(d_pre_node, w_node[...])
    sums2[...] = jnp.zeros(sums2.shape, F32)
    start_all(node_outs)

    def back(index, carry):
        start = pl.multiple_of(index * MAIN_ROWS, MAIN_ROWS)
        hit = jnp.concatenate(
            [pick(block_rows(recv, index, part), d_agg.shape[0]) for part in range(parts)], axis=0
        )
        d_sent = mm(hit, d_agg[...])
        outs = []
        for low in range(0, MAIN_ROWS, CHUNK):
            if low % COPY == 0:
                block_in(2, index * ratio + low // COPY).wait()
            here = pl.ds(start + low, CHUNK)
            if low % BLOCK == 0:
                live = jnp.where(index * parts + low // BLOCK < live_count, 1.0, 0.0)
                live_gain = edge_gain[...] * live.astype(F32)
            d_message = edge_cot[here, :].astype(F32) + d_sent[low : low + CHUNK]
            d_unit = d_message * live_gain
            outs.append(norm_back(d_unit, unit[here, :], inverse[here, :]).astype(BF))
        d_hid = mm_t(jnp.concatenate(outs, axis=0), w_edge_out[...])
        pres = []
        for low in range(0, MAIN_ROWS, CHUNK):
            here = pl.ds(start + low, CHUNK)
            part = (d_hid[low : low + CHUNK] * slope[here, :]).astype(BF)
            d_pre[here, :] = part
            pres.append(part)
            if (low + CHUNK) % COPY == 0:
                block_out(1, index * ratio + low // COPY).start()
        hit_t = jnp.concatenate(
            [
                pick_t(
                    remote_index(block_rows(send, index, part), own, near_rows, peers, shift),
                    height,
                )
                for part in range(parts)
            ],
            axis=1,
        )
        sums2[...] += mm(hit_t, jnp.concatenate(pres, axis=0))
        return carry

    lax.fori_loop(0, blocks, back, 0)

    d_rows2 = mm_t(sums2[...].astype(BF), w_send[...])
    for index in range(steps):
        near_out[index][...] = d_rows2[index * near_width : (index + 1) * near_width].astype(BF)
    d_coarse = None
    for slot in range(far_width):
        start = near_rows + slot * peers
        term = mm(far_hits[slot], d_rows2[start : start + peers].astype(BF))
        d_coarse = term if d_coarse is None else d_coarse + term
    far_out[...] = d_coarse.astype(BF)
    for index in range(copies):
        block_out(0, index).wait()
        block_out(1, index).wait()
    wait_all(node_outs)


def local_back_kernel(*refs):
    sources, block_sources = refs[:7], refs[7:9]
    edge_grad_out, node_sum, near_hit = refs[9:12]
    targets, block_targets = refs[12:19], refs[19:21]
    edge_grad, sums, load, store = refs[21:]
    send, recv, w_edge, w_send, w_recv, d_node, lists = targets
    d_pre, cot = block_targets
    own = d_node.shape[0]
    parts = ROWS // LANES
    copies = d_pre.shape[0] // COPY
    ratio = ROWS // COPY
    fixed = copies_of(sources, targets, load)

    def block_in(which, index):
        here = rows_of(index)
        return pltpu.make_async_copy(
            block_sources[which].at[here, :],
            block_targets[which].at[here, :],
            load.at[7 + which * copies + index],
        )

    def block_out(index):
        here = rows_of(index)
        return pltpu.make_async_copy(edge_grad.at[here, :], edge_grad_out.at[here, :], store.at[index])

    start_all(fixed[:3])
    for index in range(copies):
        block_in(0, index).start()
        block_in(1, index).start()
    start_all(fixed[3:])
    sums[...] = jnp.zeros(sums.shape, F32)
    wait_all(fixed[:3])

    def step(index, carry):
        here = pl.ds(pl.multiple_of(index * ROWS, ROWS), ROWS)
        hit = jnp.concatenate(
            [
                own_pick_t(
                    send[pl.ds(index * parts + part, 1), :],
                    recv[pl.ds(index * parts + part, 1), :],
                    own,
                )
                for part in range(parts)
            ],
            axis=1,
        )
        for part in range(ratio):
            block_in(0, index * ratio + part).wait()
            block_in(1, index * ratio + part).wait()
        grads = d_pre[here, :]
        value = cot[here, :].astype(F32) + mm_t(grads, w_edge[...])
        edge_grad[here, :] = value.astype(BF)
        for part in range(ratio):
            block_out(index * ratio + part).start()
        sums[...] += mm(hit, grads)
        return carry

    lax.fori_loop(0, d_pre.shape[0] // ROWS, step, 0)
    wait_all(fixed[3:])
    total = sums[...].astype(BF)
    node_sum[...] = d_node[...] + mm_t(total[:own], w_send[...]) + mm_t(total[own:], w_recv[...])
    steps, width = lists.shape
    ids = lax.broadcasted_iota(jnp.int32, (own, width), 0)
    near_hit[...] = jnp.concatenate(
        [ones_where(ids == lists[index : index + 1, :]) for index in range(steps)], axis=1
    )
    for index in range(copies):
        block_out(index).wait()


def combine_kernel(coarse, node_sum, hit, far, *refs):
    steps = len(refs) - 2
    near = jnp.concatenate([ref[...] for ref in refs[:steps]], axis=0)
    out, total = refs[steps], refs[steps + 1]
    total[...] = node_sum[...] + mm(hit[...], near)
    peers, count, _ = far.shape
    grads = far[0].astype(F32)
    for index in range(1, peers):
        grads = grads + far[index].astype(F32)
    for index in range(count):
        here = pl.ds(coarse[index], 1)
        total[here, :] = total[here, :] + grads[index : index + 1]
    out[...] = total[...].astype(BF)


def vmem(count):
    return [pl.BlockSpec(memory_space=pltpu.VMEM) for _ in range(count)]


def hbm(count):
    return [pl.BlockSpec(memory_space=pltpu.HBM) for _ in range(count)]


def smem():
    return pl.BlockSpec(memory_space=pltpu.SMEM)


def local(
    nodes,
    edges,
    node_cot,
    edge_cot,
    w_edge,
    w_send,
    w_recv,
    edge_bias,
    w_edge_out,
    edge_out_bias,
    edge_gain,
    w_node,
    w_agg,
    node_bias,
    w_node_out,
    node_out_bias,
    node_gain,
    send_slots,
    recv_slots,
    neighbour_send_lists,
    coarse_rows,
    far_lists,
    block_count,
):
    own, width = nodes.shape
    hidden = w_edge.shape[1]
    edge_rows = edges.shape[0]
    peers = lax.axis_size("patch")
    steps, near_width = neighbour_send_lists.shape
    offsets = [(index // 2 + 1) * (1 - 2 * (index % 2)) for index in range(steps)]
    coarse_count = coarse_rows.shape[0]
    far_width = far_lists.shape[2]
    shift = far_width.bit_length() - 1
    if far_width != 1 << shift or own % 64 or edge_rows % ROWS or edge_rows % MAIN_ROWS or hidden != width:
        raise ValueError("unsupported sizes")
    slots = steps * near_width + peers * far_width
    height = -(-slots // LANES) * LANES
    own_pad = -(-own // LANES) * LANES
    send = send_slots.reshape(-1, LANES)
    recv = recv_slots.reshape(-1, LANES)
    blocks = edge_rows // ROWS
    copies = edge_rows // COPY
    row = lambda value: value.reshape(1, -1)
    shape = jax.ShapeDtypeStruct

    small = lambda: pltpu.VMEM((1, width), F32)
    square = lambda: pltpu.VMEM((width, hidden), BF)
    index_rows = lambda: pltpu.VMEM((edge_rows // LANES, LANES), jnp.int32)
    edge_like = lambda: pltpu.VMEM((edge_rows, width), BF)
    node_like = lambda: pltpu.VMEM((own, width), BF)
    here = lambda value: pltpu.with_memory_space_constraint(value, pltpu.VMEM)

    packed = pl.pallas_call(
        pack_kernel,
        out_shape=[pltpu.VMEM((near_width, width), BF)] * steps
        + [pltpu.VMEM((peers, coarse_count, width), BF)],
        in_specs=vmem(3),
        out_specs=vmem(steps + 1),
        name="pack",
    )(nodes, neighbour_send_lists, row(coarse_rows))
    near = [here(passed_along(packed[index], "patch", offsets[index])) for index in range(steps)]
    coarse = here(
        lax.all_to_all(packed[steps], "patch", split_axis=0, concat_axis=0, tiled=True).reshape(
            -1, width
        )
    )

    pre_local = pl.pallas_call(
        local_kernel,
        out_shape=shape((edge_rows, hidden), BF),
        in_specs=hbm(8),
        out_specs=hbm(1)[0],
        scratch_shapes=[
            node_like(),
            square(),
            square(),
            index_rows(),
            index_rows(),
            square(),
            small(),
            edge_like(),
            pltpu.VMEM((2 * own, hidden), BF),
            edge_like(),
            pltpu.SemaphoreType.DMA((7 + copies,)),
            pltpu.SemaphoreType.DMA((copies,)),
        ],
        cost_estimate=pl.CostEstimate(
            flops=2 * edge_rows * width * hidden * 3, transcendentals=0, bytes_accessed=6 << 20
        ),
        name="local_ahead",
    )(nodes, w_send, w_recv, send, recv, w_edge, row(edge_bias), edges)

    outs = pl.pallas_call(
        lambda *refs: main_kernel(shift, steps, *refs),
        out_shape=[pltpu.VMEM((near_width, width), BF)] * steps
        + [
            pltpu.VMEM((peers * coarse_count, width), BF),
            shape((own, width), BF),
            shape((own, width), F32),
            shape((edge_rows, width), BF),
            shape((edge_rows, hidden), BF),
        ],
        in_specs=[smem()] + vmem(1 + steps) + hbm(FIXED + 3),
        out_specs=vmem(1 + steps) + hbm(4),
        scratch_shapes=[
            pltpu.VMEM((far_width, peers), jnp.int32),
            square(),
            index_rows(),
            index_rows(),
            square(),
            small(),
            small(),
            node_like(),
            square(),
            square(),
            small(),
            square(),
            small(),
            node_like(),
            small(),
            edge_like(),
            edge_like(),
            edge_like(),
            node_like(),
            pltpu.VMEM((own, width), F32),
            edge_like(),
            edge_like(),
            pltpu.VMEM((height, width), BF),
            pltpu.VMEM((height, hidden), BF),
            pltpu.VMEM((edge_rows, hidden), F32),
            pltpu.VMEM((edge_rows, width), F32),
            pltpu.VMEM((edge_rows, 1), F32),
            pltpu.VMEM((own, width), F32),
            pltpu.VMEM((own_pad, width), BF),
            pltpu.VMEM((height, hidden), F32),
            pltpu.SemaphoreType.DMA((FIXED + 3 * copies,)),
            pltpu.SemaphoreType.DMA((2 * copies + 2,)),
        ],
        cost_estimate=pl.CostEstimate(
            flops=2 * edge_rows * width * hidden * 8, transcendentals=0, bytes_accessed=16 << 20
        ),
        name="main",
    )(
        block_count,
        *near,
        coarse,
        far_lists[0].T,
        w_send,
        send,
        recv,
        w_edge_out,
        row(edge_out_bias),
        row(edge_gain),
        nodes,
        w_agg,
        w_node,
        row(node_bias),
        w_node_out,
        row(node_out_bias),
        node_cot,
        row(node_gain),
        pre_local,
        edges,
        edge_cot,
    )
    new_nodes, d_node, new_edges, d_pre = outs[1 + steps :]
    returned = [
        here(passed_along(outs[index], "patch", -offsets[index])) for index in range(steps)
    ]
    far_back = here(
        lax.all_to_all(
            outs[steps].reshape(peers, coarse_count, width),
            "patch",
            split_axis=0,
            concat_axis=0,
            tiled=True,
        )
    )

    edge_grad, node_sum, near_hit = pl.pallas_call(
        local_back_kernel,
        out_shape=[
            shape((edge_rows, width), BF),
            pltpu.VMEM((own, width), F32),
            pltpu.VMEM((own, steps * near_width), BF),
        ],
        in_specs=hbm(9),
        out_specs=hbm(1) + vmem(2),
        scratch_shapes=[
            index_rows(),
            index_rows(),
            square(),
            square(),
            square(),
            pltpu.VMEM((own, width), F32),
            pltpu.VMEM((steps, near_width), jnp.int32),
            edge_like(),
            edge_like(),
            edge_like(),
            pltpu.VMEM((2 * own, hidden), F32),
            pltpu.SemaphoreType.DMA((7 + 2 * copies,)),
            pltpu.SemaphoreType.DMA((copies,)),
        ],
        cost_estimate=pl.CostEstimate(
            flops=2 * edge_rows * width * hidden * 3, transcendentals=0, bytes_accessed=6 << 20
        ),
        name="local_back",
    )(send, recv, w_edge, w_send, w_recv, d_node, neighbour_send_lists, d_pre, edge_cot)

    node_grad = pl.pallas_call(
        combine_kernel,
        out_shape=shape((own, width), BF),
        in_specs=[smem()] + vmem(3 + steps),
        out_specs=vmem(1)[0],
        scratch_shapes=[pltpu.VMEM((own, width), F32)],
        name="combine",
    )(coarse_rows, node_sum, near_hit, far_back, *returned)
    return new_nodes, new_edges, node_grad, edge_grad


def solution(mesh):
    rows = P(("groups", "patch"), None)
    placed = (
        (rows,) * 4
        + (P(),) * 13
        + (
            P("patch"),
            P("patch"),
            P("patch", None),
            P("patch"),
            P("patch", None, None),
            P("patch"),
        )
    )
    return jax.shard_map(
        local,
        mesh=mesh,
        in_specs=placed,
        out_specs=(rows,) * 4,
        check_vma=False,
    )
```

```python
import jax
import jax.numpy as jnp
from jax import lax
from jax.experimental import pallas as pl
from jax.experimental.pallas import tpu as pltpu
from jax.sharding import PartitionSpec as P

BLOCK = 128
LANES = 128
ROWS = 512
MAIN_ROWS = 1536
COPY = 256
CHUNK = 16
FIXED = 15
EPS = 1e-05
BF = jnp.bfloat16
F32 = jnp.float32


def swapped(value, axis, bit, shift):
    count = lax.axis_size(axis)
    pairs = [(source, (((source + shift) ^ bit) - shift) % count) for source in range(count)]
    return lax.ppermute(value, axis, pairs)


def mm(a, b):
    return lax.dot_general(a, b, (((1,), (0,)), ((), ())), preferred_element_type=F32)


def mm_t(a, b):
    return lax.dot_general(a, b, (((1,), (1,)), ((), ())), preferred_element_type=F32)


def mm_l(a, b):
    return lax.dot_general(a, b, (((0,), (0,)), ((), ())), preferred_element_type=F32)


def ones_where(mask):
    return jnp.where(mask, 1.0, 0.0).astype(BF)


def as_columns(row):
    return jnp.broadcast_to(row.astype(F32), (LANES, LANES)).T.astype(jnp.int32)


def lane_ids(tile):
    return lax.broadcasted_iota(jnp.int32, (LANES, LANES), 1) + tile * LANES


def own_pick(send, recv, own):
    sender = as_columns(jnp.where(send < own, send, -1))
    receiver = as_columns(recv + own)
    tiles = []
    for tile in range(2 * own // LANES):
        ids = lane_ids(tile)
        if (tile + 1) * LANES <= own:
            hit = sender == ids
        elif tile * LANES >= own:
            hit = receiver == ids
        else:
            hit = (sender == ids) | (receiver == ids)
        tiles.append(ones_where(hit))
    return jnp.concatenate(tiles, axis=1)


def own_pick_t(send, recv, own):
    sender = jnp.where(send < own, send, -1)
    ids = lax.broadcasted_iota(jnp.int32, (own, LANES), 0)
    return jnp.concatenate([ones_where(ids == sender), ones_where(ids == recv)], axis=0)


def remote_index(send, own, near, peers, shift):
    far = send - (own + near)
    far_index = near + (far & ((1 << shift) - 1)) * peers + (far >> shift)
    return jnp.where(send < own + near, send - own, far_index)


def pick(row, width):
    column = as_columns(row)
    return jnp.concatenate(
        [ones_where(column == lane_ids(tile)) for tile in range(width // LANES)], axis=1
    )


def pick_t(row, height):
    return ones_where(lax.broadcasted_iota(jnp.int32, (height, LANES), 0) == row)


def silu_parts(value):
    gate = 0.5 * jnp.tanh(0.5 * value) + 0.5
    hidden = value * gate
    slope = gate * (1.0 + value - hidden)
    return hidden, slope


def norm_parts(value):
    center = value - jnp.mean(value, axis=-1, keepdims=True)
    inverse = lax.rsqrt(jnp.mean(center * center, axis=-1, keepdims=True) + EPS)
    return center * inverse, inverse


def norm_back(grad, unit, inverse):
    first = jnp.mean(grad, axis=-1, keepdims=True)
    second = jnp.mean(grad * unit, axis=-1, keepdims=True)
    return inverse * (grad - first - unit * second)


def copies_of(sources, targets, sems):
    return [
        pltpu.make_async_copy(source, target, sems.at[index])
        for index, (source, target) in enumerate(zip(sources, targets))
    ]


def start_all(copies):
    for copy in copies:
        copy.start()


def wait_all(copies):
    for copy in copies:
        copy.wait()


def rows_of(index):
    return pl.ds(pl.multiple_of(index * COPY, COPY), COPY)


def place():
    index = lax.axis_index("patch")
    return index & 1, (index >> 1) & 1


def pack_kernel(nodes, lists, coarse, pair_out, first_out, second_out, out):
    rows = nodes[...]
    own = rows.shape[0]
    width = lists.shape[1]
    _, odd = place()
    ids = lax.broadcasted_iota(jnp.int32, (own, width), 0)

    def picked(index):
        return mm_l(ones_where(ids == lists[pl.ds(index, 1), :]), rows).astype(BF)

    pair_out[:width] = picked(odd)
    pair_out[width:] = picked(1 - odd)
    first_out[...] = picked(2 + odd)
    second_out[...] = picked(3 - odd)
    count = coarse.shape[1]
    hit = ones_where(lax.broadcasted_iota(jnp.int32, (own, count), 0) == coarse[...])
    chosen = mm_l(hit, rows).astype(BF)

    def put(index, carry):
        out[index] = chosen
        return carry

    lax.fori_loop(0, out.shape[0], put, 0)


def join_kernel(relay, pair, first, second, first_out, second_out):
    width = first.shape[0]
    first_out[:width] = first[...]
    first_out[width:] = pair[relay[0] * width : (relay[0] + 1) * width]
    second_out[:width] = second[...]
    second_out[width:] = pair[relay[1] * width : (relay[1] + 1) * width]


def local_kernel(*refs):
    sources, edges_in, out = refs[:7], refs[7], refs[8]
    targets, edges, table, value, load, store = refs[9:16], *refs[16:]
    nodes, w_send, w_recv, send, recv, w_edge, bias = targets
    own = nodes.shape[0]
    parts = ROWS // LANES
    copies = edges.shape[0] // COPY
    ratio = ROWS // COPY
    fixed = copies_of(sources, targets, load)

    def block_in(index):
        here = rows_of(index)
        return pltpu.make_async_copy(edges_in.at[here, :], edges.at[here, :], load.at[7 + index])

    def block_out(index):
        here = rows_of(index)
        return pltpu.make_async_copy(value.at[here, :], out.at[here, :], store.at[index])

    start_all(fixed)
    for index in range(copies):
        block_in(index).start()
    wait_all(fixed[:2])
    rows = nodes[...]
    table[:own] = mm(rows, w_send[...]).astype(BF)
    fixed[2].wait()
    table[own:] = mm(rows, w_recv[...]).astype(BF)
    wait_all(fixed[3:])

    def step(index, carry):
        here = pl.ds(pl.multiple_of(index * ROWS, ROWS), ROWS)
        hit = jnp.concatenate(
            [
                own_pick(
                    send[pl.ds(index * parts + part, 1), :],
                    recv[pl.ds(index * parts + part, 1), :],
                    own,
                )
                for part in range(parts)
            ],
            axis=0,
        )
        near = mm(hit, table[...]) + bias[...]
        for part in range(ratio):
            block_in(index * ratio + part).wait()
        value[here, :] = (near + mm(edges[here, :], w_edge[...])).astype(BF)
        for part in range(ratio):
            block_out(index * ratio + part).start()
        return carry

    lax.fori_loop(0, edges.shape[0] // ROWS, step, 0)
    for index in range(copies):
        block_out(index).wait()


def main_kernel(shift, steps, *refs):
    take = iter(refs)
    count = next(take)
    received = [next(take) for _ in range(3)]
    coarse = next(take)
    sources = [next(take) for _ in range(FIXED)]
    block_sources = [next(take) for _ in range(3)]
    pair_out, first_out, second_out, far_out = [next(take) for _ in range(4)]
    new_nodes_out, d_node_out, new_edges_out, d_pre_out = [next(take) for _ in range(4)]
    targets = [next(take) for _ in range(FIXED)]
    pre_in, edges, edge_cot = block_targets = [next(take) for _ in range(3)]
    new_nodes, d_node, new_edges, d_pre = [next(take) for _ in range(4)]
    stack, rows2, table2, slope, unit, inverse, agg, d_agg, sums2 = [next(take) for _ in range(9)]
    load, store = next(take), next(take)
    far_lists, w_send, send, recv, w_edge_out, edge_out_bias, edge_gain = targets[:7]
    nodes, w_agg, w_node, node_bias, w_node_out, node_out_bias, node_cot, node_gain = targets[7:]
    own = nodes.shape[0]
    width = nodes.shape[1]
    far_width, peers = far_lists.shape
    near_width = first_out.shape[0]
    core, odd = place()
    near_rows = steps * near_width
    height = table2.shape[0]
    coarse_rows = coarse.shape[0] // peers
    parts = MAIN_ROWS // LANES
    blocks = edges.shape[0] // MAIN_ROWS
    copies = edges.shape[0] // COPY
    ratio = MAIN_ROWS // COPY
    live_count = count[0]
    fixed = copies_of(sources, targets, load)

    def block_in(which, index):
        here = rows_of(index)
        return pltpu.make_async_copy(
            block_sources[which].at[here, :],
            block_targets[which].at[here, :],
            load.at[FIXED + which * copies + index],
        )

    def block_out(which, index):
        here = rows_of(index)
        source, target = ((new_edges, new_edges_out), (d_pre, d_pre_out))[which]
        return pltpu.make_async_copy(
            source.at[here, :], target.at[here, :], store.at[which * copies + index]
        )

    node_outs = [
        pltpu.make_async_copy(new_nodes, new_nodes_out, store.at[2 * copies]),
        pltpu.make_async_copy(d_node, d_node_out, store.at[2 * copies + 1]),
    ]
    start_all(fixed[:4])
    block_in(0, 0).start()
    start_all(fixed[4:7])
    block_in(1, 0).start()
    for index in range(1, copies):
        block_in(0, index).start()
        block_in(1, index).start()
    start_all(fixed[7:])
    for index in range(copies):
        block_in(2, index).start()

    fixed[0].wait()
    far_ids = lax.broadcasted_iota(jnp.int32, (coarse.shape[0], peers), 0)
    far_base = lax.broadcasted_iota(jnp.int32, (coarse.shape[0], peers), 1) * coarse_rows
    far_hits = [
        ones_where(far_ids == far_base + far_lists[slot : slot + 1, :])
        for slot in range(far_width)
    ]
    rows2[...] = jnp.zeros(rows2.shape, BF)
    for index, ref in enumerate(received):
        stack[2 * index * near_width : 2 * (index + 1) * near_width] = ref[...]
    below = 4 - 2 * odd
    above = 2 + 2 * odd
    chosen = [
        jnp.where(core == 0, below + 1, odd),
        jnp.where(core == 0, 1 - odd, above + 1),
        below,
        above,
    ]
    for index, slot in enumerate(chosen):
        start = pl.multiple_of(slot * near_width, near_width)
        rows2[index * near_width : (index + 1) * near_width] = stack[pl.ds(start, near_width), :]
    for slot in range(far_width):
        start = near_rows + slot * peers
        rows2[start : start + peers] = mm_l(far_hits[slot], coarse[...]).astype(BF)
    fixed[1].wait()
    table2[...] = mm(rows2[...], w_send[...]).astype(BF)
    wait_all(fixed[2:4])
    agg[...] = jnp.zeros(agg.shape, F32)
    wait_all(fixed[4:7])

    def block_rows(ref, index, part):
        return ref[pl.ds(index * parts + part, 1), :]

    def ahead(index, carry):
        start = pl.multiple_of(index * MAIN_ROWS, MAIN_ROWS)
        hit = jnp.concatenate(
            [
                pick(remote_index(block_rows(send, index, part), own, near_rows, peers, shift), height)
                for part in range(parts)
            ],
            axis=0,
        )
        remote = mm(hit, table2[...])
        hidden = []
        for low in range(0, MAIN_ROWS, CHUNK):
            if low % COPY == 0:
                block_in(0, index * ratio + low // COPY).wait()
            here = pl.ds(start + low, CHUNK)
            value = pre_in[here, :].astype(F32) + remote[low : low + CHUNK]
            part_hidden, part_slope = silu_parts(value)
            slope[here, :] = part_slope
            hidden.append(part_hidden.astype(BF))
        out = mm(jnp.concatenate(hidden, axis=0), w_edge_out[...])
        sent = []
        for low in range(0, MAIN_ROWS, CHUNK):
            if low % COPY == 0:
                block_in(1, index * ratio + low // COPY).wait()
            here = pl.ds(start + low, CHUNK)
            if low % BLOCK == 0:
                live = jnp.where(index * parts + low // BLOCK < live_count, 1.0, 0.0)
                live_gain = edge_gain[...] * live.astype(F32)
            part_unit, part_inverse = norm_parts(out[low : low + CHUNK] + edge_out_bias[...])
            unit[here, :] = part_unit
            inverse[here, :] = part_inverse
            message = part_unit * live_gain
            new_edges[here, :] = (edges[here, :].astype(F32) + message).astype(BF)
            sent.append(message.astype(BF))
            if (low + CHUNK) % COPY == 0:
                block_out(0, index * ratio + low // COPY).start()
        hit_t = jnp.concatenate(
            [pick_t(block_rows(recv, index, part), own) for part in range(parts)], axis=1
        )
        agg[...] += mm(hit_t, jnp.concatenate(sent, axis=0))
        return carry

    lax.fori_loop(0, blocks, ahead, 0)

    wait_all(fixed[7:])
    rows = nodes[...]
    pre_node = mm(rows, w_node[...]) + mm(agg[...].astype(BF), w_agg[...]) + node_bias[...]
    node_hidden, node_slope = silu_parts(pre_node)
    node_out = mm(node_hidden.astype(BF), w_node_out[...]) + node_out_bias[...]
    node_unit, node_inverse = norm_parts(node_out)
    new_nodes[...] = (rows.astype(F32) + node_gain[...] * node_unit).astype(BF)
    cot = node_cot[...].astype(F32)
    d_out = norm_back(cot * node_gain[...], node_unit, node_inverse).astype(BF)
    d_hidden = mm_t(d_out, w_node_out[...]).astype(BF).astype(F32)
    d_pre_node = (d_hidden * node_slope).astype(BF)
    d_agg[...] = jnp.zeros(d_agg.shape, BF)
    d_agg[:own] = mm_t(d_pre_node, w_agg[...]).astype(BF)
    d_node[...] = cot + mm_t(d_pre_node, w_node[...])
    sums2[...] = jnp.zeros(sums2.shape, F32)
    start_all(node_outs)

    def back(index, carry):
        start = pl.multiple_of(index * MAIN_ROWS, MAIN_ROWS)
        hit = jnp.concatenate(
            [pick(block_rows(recv, index, part), d_agg.shape[0]) for part in range(parts)], axis=0
        )
        d_sent = mm(hit, d_agg[...])
        outs = []
        for low in range(0, MAIN_ROWS, CHUNK):
            if low % COPY == 0:
                block_in(2, index * ratio + low // COPY).wait()
            here = pl.ds(start + low, CHUNK)
            if low % BLOCK == 0:
                live = jnp.where(index * parts + low // BLOCK < live_count, 1.0, 0.0)
                live_gain = edge_gain[...] * live.astype(F32)
            d_message = edge_cot[here, :].astype(F32) + d_sent[low : low + CHUNK]
            d_unit = d_message * live_gain
            outs.append(norm_back(d_unit, unit[here, :], inverse[here, :]).astype(BF))
        d_hid = mm_t(jnp.concatenate(outs, axis=0), w_edge_out[...])
        pres = []
        for low in range(0, MAIN_ROWS, CHUNK):
            here = pl.ds(start + low, CHUNK)
            part = (d_hid[low : low + CHUNK] * slope[here, :]).astype(BF)
            d_pre[here, :] = part
            pres.append(part)
            if (low + CHUNK) % COPY == 0:
                block_out(1, index * ratio + low // COPY).start()
        hit_t = jnp.concatenate(
            [
                pick_t(
                    remote_index(block_rows(send, index, part), own, near_rows, peers, shift),
                    height,
                )
                for part in range(parts)
            ],
            axis=1,
        )
        sums2[...] += mm(hit_t, jnp.concatenate(pres, axis=0))
        return carry

    lax.fori_loop(0, blocks, back, 0)

    d_rows2 = mm_t(sums2[...].astype(BF), w_send[...])
    stack[: steps * near_width] = d_rows2[: steps * near_width].astype(BF)
    outgoing = [
        (pair_out, 0, 1 - core),
        (pair_out, 1, core),
        (first_out, 0, 3 - odd),
        (second_out, 0, 2 + odd),
    ]
    for ref, index, slot in outgoing:
        start = pl.multiple_of(slot * near_width, near_width)
        ref[index * near_width : (index + 1) * near_width] = stack[pl.ds(start, near_width), :]
    d_coarse = None
    for slot in range(far_width):
        start = near_rows + slot * peers
        term = mm(far_hits[slot], d_rows2[start : start + peers].astype(BF))
        d_coarse = term if d_coarse is None else d_coarse + term
    far_out[...] = d_coarse.astype(BF)
    for index in range(copies):
        block_out(0, index).wait()
        block_out(1, index).wait()
    wait_all(node_outs)


def local_back_kernel(*refs):
    sources, block_sources = refs[:7], refs[7:9]
    edge_grad_out, node_sum, near_hit = refs[9:12]
    targets, block_targets = refs[12:19], refs[19:21]
    edge_grad, sums, load, store = refs[21:]
    send, recv, w_edge, w_send, w_recv, d_node, lists = targets
    d_pre, cot = block_targets
    own = d_node.shape[0]
    parts = ROWS // LANES
    copies = d_pre.shape[0] // COPY
    ratio = ROWS // COPY
    fixed = copies_of(sources, targets, load)

    def block_in(which, index):
        here = rows_of(index)
        return pltpu.make_async_copy(
            block_sources[which].at[here, :],
            block_targets[which].at[here, :],
            load.at[7 + which * copies + index],
        )

    def block_out(index):
        here = rows_of(index)
        return pltpu.make_async_copy(edge_grad.at[here, :], edge_grad_out.at[here, :], store.at[index])

    start_all(fixed[:3])
    for index in range(copies):
        block_in(0, index).start()
        block_in(1, index).start()
    start_all(fixed[3:])
    sums[...] = jnp.zeros(sums.shape, F32)
    wait_all(fixed[:3])

    def step(index, carry):
        here = pl.ds(pl.multiple_of(index * ROWS, ROWS), ROWS)
        hit = jnp.concatenate(
            [
                own_pick_t(
                    send[pl.ds(index * parts + part, 1), :],
                    recv[pl.ds(index * parts + part, 1), :],
                    own,
                )
                for part in range(parts)
            ],
            axis=1,
        )
        for part in range(ratio):
            block_in(0, index * ratio + part).wait()
            block_in(1, index * ratio + part).wait()
        grads = d_pre[here, :]
        value = cot[here, :].astype(F32) + mm_t(grads, w_edge[...])
        edge_grad[here, :] = value.astype(BF)
        for part in range(ratio):
            block_out(index * ratio + part).start()
        sums[...] += mm(hit, grads)
        return carry

    lax.fori_loop(0, d_pre.shape[0] // ROWS, step, 0)
    wait_all(fixed[3:])
    total = sums[...].astype(BF)
    node_sum[...] = d_node[...] + mm_t(total[:own], w_send[...]) + mm_t(total[own:], w_recv[...])
    width = lists.shape[1]
    ids = lax.broadcasted_iota(jnp.int32, (own, width), 0)
    core, odd = place()
    same = jnp.where(core == odd, 0, 2 * own)
    other = jnp.where(core == odd, 2 * own, 0)
    hits = [(core, 0), (2 + odd, 0), (odd, other), (3 - odd, 0), (1 - odd, same)]
    near_hit[...] = jnp.concatenate(
        [ones_where(ids == lists[pl.ds(index, 1), :] + away) for index, away in hits], axis=1
    )
    for index in range(copies):
        block_out(index).wait()


def combine_kernel(coarse, node_sum, hit, far, pair, first, second, out, total):
    width = pair.shape[0] // 2
    near = jnp.concatenate([pair[:width], first[...], second[...]], axis=0)
    total[...] = node_sum[...] + mm(hit[...], near)
    peers, count, _ = far.shape
    grads = far[0].astype(F32)
    for index in range(1, peers):
        grads = grads + far[index].astype(F32)
    for index in range(count):
        here = pl.ds(coarse[index], 1)
        total[here, :] = total[here, :] + grads[index : index + 1]
    out[...] = total[...].astype(BF)


def vmem(count):
    return [pl.BlockSpec(memory_space=pltpu.VMEM) for _ in range(count)]


def hbm(count):
    return [pl.BlockSpec(memory_space=pltpu.HBM) for _ in range(count)]


def smem():
    return pl.BlockSpec(memory_space=pltpu.SMEM)


def local(
    nodes,
    edges,
    node_cot,
    edge_cot,
    w_edge,
    w_send,
    w_recv,
    edge_bias,
    w_edge_out,
    edge_out_bias,
    edge_gain,
    w_node,
    w_agg,
    node_bias,
    w_node_out,
    node_out_bias,
    node_gain,
    send_slots,
    recv_slots,
    neighbour_send_lists,
    coarse_rows,
    far_lists,
    block_count,
):
    own, width = nodes.shape
    hidden = w_edge.shape[1]
    edge_rows = edges.shape[0]
    peers = lax.axis_size("patch")
    steps, near_width = neighbour_send_lists.shape
    coarse_count = coarse_rows.shape[0]
    far_width = far_lists.shape[2]
    shift = far_width.bit_length() - 1
    if steps != 4 or peers % 4 or far_width != 1 << shift or own % 64 or edge_rows % ROWS or edge_rows % MAIN_ROWS or hidden != width:
        raise ValueError("unsupported sizes")
    slots = steps * near_width + peers * far_width
    height = -(-slots // LANES) * LANES
    own_pad = -(-own // LANES) * LANES
    send = send_slots.reshape(-1, LANES)
    recv = recv_slots.reshape(-1, LANES)
    blocks = edge_rows // ROWS
    copies = edge_rows // COPY
    row = lambda value: value.reshape(1, -1)
    shape = jax.ShapeDtypeStruct

    small = lambda: pltpu.VMEM((1, width), F32)
    square = lambda: pltpu.VMEM((width, hidden), BF)
    index_rows = lambda: pltpu.VMEM((edge_rows // LANES, LANES), jnp.int32)
    edge_like = lambda: pltpu.VMEM((edge_rows, width), BF)
    node_like = lambda: pltpu.VMEM((own, width), BF)
    here = lambda value: pltpu.with_memory_space_constraint(value, pltpu.VMEM)

    near_like = pltpu.VMEM((near_width, width), BF)
    pair_like = pltpu.VMEM((2 * near_width, width), BF)

    def exchanged(pair, first, second, rows, relay):
        pair = here(swapped(pair, "patch", 1, 0))
        rows = lax.all_to_all(rows, "patch", split_axis=0, concat_axis=0, tiled=True)
        first, second = pl.pallas_call(
            lambda *refs: join_kernel(relay, *refs),
            out_shape=[pair_like] * 2,
            in_specs=vmem(3),
            out_specs=vmem(2),
            name="join",
        )(pair, here(first), here(second))
        first = here(swapped(first, "patch", 2, 0))
        second = here(swapped(second, "patch", 2, 2))
        return pair, first, second, rows

    packed = pl.pallas_call(
        pack_kernel,
        out_shape=[pair_like, near_like, near_like, pltpu.VMEM((peers, coarse_count, width), BF)],
        in_specs=vmem(3),
        out_specs=vmem(4),
        name="pack",
    )(nodes, neighbour_send_lists, row(coarse_rows))
    *near, coarse = exchanged(*packed, (0, 1))

    pre_local = pl.pallas_call(
        local_kernel,
        out_shape=shape((edge_rows, hidden), BF),
        in_specs=hbm(8),
        out_specs=hbm(1)[0],
        scratch_shapes=[
            node_like(),
            square(),
            square(),
            index_rows(),
            index_rows(),
            square(),
            small(),
            edge_like(),
            pltpu.VMEM((2 * own, hidden), BF),
            edge_like(),
            pltpu.SemaphoreType.DMA((7 + copies,)),
            pltpu.SemaphoreType.DMA((copies,)),
        ],
        cost_estimate=pl.CostEstimate(
            flops=2 * edge_rows * width * hidden * 3, transcendentals=0, bytes_accessed=6 << 20
        ),
        name="local_ahead",
    )(nodes, w_send, w_recv, send, recv, w_edge, row(edge_bias), edges)

    outs = pl.pallas_call(
        lambda *refs: main_kernel(shift, steps, *refs),
        out_shape=[
            pair_like,
            near_like,
            near_like,
            pltpu.VMEM((peers * coarse_count, width), BF),
            shape((own, width), BF),
            shape((own, width), F32),
            shape((edge_rows, width), BF),
            shape((edge_rows, hidden), BF),
        ],
        in_specs=[smem()] + vmem(4) + hbm(FIXED + 3),
        out_specs=vmem(4) + hbm(4),
        scratch_shapes=[
            pltpu.VMEM((far_width, peers), jnp.int32),
            square(),
            index_rows(),
            index_rows(),
            square(),
            small(),
            small(),
            node_like(),
            square(),
            square(),
            small(),
            square(),
            small(),
            node_like(),
            small(),
            edge_like(),
            edge_like(),
            edge_like(),
            node_like(),
            pltpu.VMEM((own, width), F32),
            edge_like(),
            edge_like(),
            pltpu.VMEM((6 * near_width, width), BF),
            pltpu.VMEM((height, width), BF),
            pltpu.VMEM((height, hidden), BF),
            pltpu.VMEM((edge_rows, hidden), F32),
            pltpu.VMEM((edge_rows, width), F32),
            pltpu.VMEM((edge_rows, 1), F32),
            pltpu.VMEM((own, width), F32),
            pltpu.VMEM((own_pad, width), BF),
            pltpu.VMEM((height, hidden), F32),
            pltpu.SemaphoreType.DMA((FIXED + 3 * copies,)),
            pltpu.SemaphoreType.DMA((2 * copies + 2,)),
        ],
        cost_estimate=pl.CostEstimate(
            flops=2 * edge_rows * width * hidden * 8, transcendentals=0, bytes_accessed=16 << 20
        ),
        name="main",
    )(
        block_count,
        *near,
        here(coarse.reshape(-1, width)),
        far_lists[0].T,
        w_send,
        send,
        recv,
        w_edge_out,
        row(edge_out_bias),
        row(edge_gain),
        nodes,
        w_agg,
        w_node,
        row(node_bias),
        w_node_out,
        row(node_out_bias),
        node_cot,
        row(node_gain),
        pre_local,
        edges,
        edge_cot,
    )
    new_nodes, d_node, new_edges, d_pre = outs[4:]
    *returned, far_back = exchanged(
        *outs[:3], outs[3].reshape(peers, coarse_count, width), (1, 1)
    )

    edge_grad, node_sum, near_hit = pl.pallas_call(
        local_back_kernel,
        out_shape=[
            shape((edge_rows, width), BF),
            pltpu.VMEM((own, width), F32),
            pltpu.VMEM((own, 5 * near_width), BF),
        ],
        in_specs=hbm(9),
        out_specs=hbm(1) + vmem(2),
        scratch_shapes=[
            index_rows(),
            index_rows(),
            square(),
            square(),
            square(),
            pltpu.VMEM((own, width), F32),
            pltpu.VMEM((steps, near_width), jnp.int32),
            edge_like(),
            edge_like(),
            edge_like(),
            pltpu.VMEM((2 * own, hidden), F32),
            pltpu.SemaphoreType.DMA((7 + 2 * copies,)),
            pltpu.SemaphoreType.DMA((copies,)),
        ],
        cost_estimate=pl.CostEstimate(
            flops=2 * edge_rows * width * hidden * 3, transcendentals=0, bytes_accessed=6 << 20
        ),
        name="local_back",
    )(send, recv, w_edge, w_send, w_recv, d_node, neighbour_send_lists, d_pre, edge_cot)

    node_grad = pl.pallas_call(
        combine_kernel,
        out_shape=shape((own, width), BF),
        in_specs=[smem()] + vmem(6),
        out_specs=vmem(1)[0],
        scratch_shapes=[pltpu.VMEM((own, width), F32)],
        name="combine",
    )(coarse_rows, here(node_sum), here(near_hit), here(far_back), *returned)
    return new_nodes, new_edges, node_grad, edge_grad


def solution(mesh):
    rows = P(("groups", "patch"), None)
    placed = (
        (rows,) * 4
        + (P(),) * 13
        + (
            P("patch"),
            P("patch"),
            P("patch", None),
            P("patch"),
            P("patch", None, None),
            P("patch"),
        )
    )
    return jax.shard_map(
        local,
        mesh=mesh,
        in_specs=placed,
        out_specs=(rows,) * 4,
        check_vma=False,
    )
```

```python
import jax
import jax.numpy as jnp
from jax import lax
from jax.experimental import pallas as pl
from jax.experimental.pallas import tpu as pltpu
from jax.sharding import PartitionSpec as P

BLOCK = 128
LANES = 128
ROWS = 512
HALVES = 2
COPY = 256
CHUNK = 16
FIXED = 16
EPS = 1e-05
BF = jnp.bfloat16
F32 = jnp.float32


def swapped(value, axis, bit, shift):
    count = lax.axis_size(axis)
    pairs = [(source, (((source + shift) ^ bit) - shift) % count) for source in range(count)]
    return lax.ppermute(value, axis, pairs)


def mm(a, b):
    return lax.dot_general(a, b, (((1,), (0,)), ((), ())), preferred_element_type=F32)


def mm_t(a, b):
    return lax.dot_general(a, b, (((1,), (1,)), ((), ())), preferred_element_type=F32)


def mm_l(a, b):
    return lax.dot_general(a, b, (((0,), (0,)), ((), ())), preferred_element_type=F32)


def ones_where(mask):
    return jnp.where(mask, 1.0, 0.0).astype(BF)


def as_columns(row):
    return jnp.broadcast_to(row.astype(F32), (LANES, LANES)).T.astype(jnp.int32)


def lane_ids(tile):
    return lax.broadcasted_iota(jnp.int32, (LANES, LANES), 1) + tile * LANES


def own_pick(send, recv, own):
    sender = as_columns(jnp.where(send < own, send, -1))
    receiver = as_columns(recv + own)
    tiles = []
    for tile in range(2 * own // LANES):
        ids = lane_ids(tile)
        if (tile + 1) * LANES <= own:
            hit = sender == ids
        elif tile * LANES >= own:
            hit = receiver == ids
        else:
            hit = (sender == ids) | (receiver == ids)
        tiles.append(ones_where(hit))
    return jnp.concatenate(tiles, axis=1)


def own_pick_t(send, recv, own):
    sender = jnp.where(send < own, send, -1)
    ids = lax.broadcasted_iota(jnp.int32, (own, LANES), 0)
    return jnp.concatenate([ones_where(ids == sender), ones_where(ids == recv)], axis=0)


def remote_index(send, own, near, peers, shift):
    far = send - (own + near)
    far_index = near + (far & ((1 << shift) - 1)) * peers + (far >> shift)
    return jnp.where(send < own + near, send - own, far_index)


def pick(row, width):
    column = as_columns(row)
    return jnp.concatenate(
        [ones_where(column == lane_ids(tile)) for tile in range(width // LANES)], axis=1
    )


def pick_t(row, height):
    return ones_where(lax.broadcasted_iota(jnp.int32, (height, LANES), 0) == row)


def silu_parts(value):
    gate = 0.5 * jnp.tanh(0.5 * value) + 0.5
    hidden = value * gate
    slope = gate * (1.0 + value - hidden)
    return hidden, slope


def norm_parts(value):
    center = value - jnp.mean(value, axis=-1, keepdims=True)
    inverse = lax.rsqrt(jnp.mean(center * center, axis=-1, keepdims=True) + EPS)
    return center * inverse, inverse


def norm_back(grad, unit, inverse):
    first = jnp.mean(grad, axis=-1, keepdims=True)
    second = jnp.mean(grad * unit, axis=-1, keepdims=True)
    return inverse * (grad - first - unit * second)


def copies_of(sources, targets, sems):
    return [
        pltpu.make_async_copy(source, target, sems.at[index])
        for index, (source, target) in enumerate(zip(sources, targets))
    ]


def start_all(copies):
    for copy in copies:
        copy.start()


def wait_all(copies):
    for copy in copies:
        copy.wait()


def rows_of(index):
    return pl.ds(pl.multiple_of(index * COPY, COPY), COPY)


def place():
    index = lax.axis_index("patch")
    return index & 1, (index >> 1) & 1


def pack_kernel(nodes, lists, coarse, pair_out, first_out, second_out, out):
    rows = nodes[...]
    own = rows.shape[0]
    width = lists.shape[1]
    _, odd = place()
    ids = lax.broadcasted_iota(jnp.int32, (own, width), 0)

    def picked(index):
        return mm_l(ones_where(ids == lists[pl.ds(index, 1), :]), rows).astype(BF)

    pair_out[:width] = picked(odd)
    pair_out[width:] = picked(1 - odd)
    first_out[...] = picked(2 + odd)
    second_out[...] = picked(3 - odd)
    count = coarse.shape[1]
    hit = ones_where(lax.broadcasted_iota(jnp.int32, (own, count), 0) == coarse[...])
    chosen = mm_l(hit, rows).astype(BF)

    def put(index, carry):
        out[index] = chosen
        return carry

    lax.fori_loop(0, out.shape[0], put, 0)


def join_kernel(relay, pair, first, second, first_out, second_out):
    width = first.shape[0]
    first_out[:width] = first[...]
    first_out[width:] = pair[relay[0] * width : (relay[0] + 1) * width]
    second_out[:width] = second[...]
    second_out[width:] = pair[relay[1] * width : (relay[1] + 1) * width]


def local_kernel(*refs):
    sources, edges_in, out = refs[:7], refs[7], refs[8]
    targets, edges, table, value, load, store = refs[9:16], *refs[16:]
    nodes, w_send, w_recv, send, recv, w_edge, bias = targets
    own = nodes.shape[0]
    parts = ROWS // LANES
    copies = edges.shape[0] // COPY
    ratio = ROWS // COPY
    fixed = copies_of(sources, targets, load)

    def block_in(index):
        here = rows_of(index)
        return pltpu.make_async_copy(edges_in.at[here, :], edges.at[here, :], load.at[7 + index])

    def block_out(index):
        here = rows_of(index)
        return pltpu.make_async_copy(value.at[here, :], out.at[here, :], store.at[index])

    start_all(fixed)
    for index in range(copies):
        block_in(index).start()
    wait_all(fixed[:2])
    rows = nodes[...]
    table[:own] = mm(rows, w_send[...]).astype(BF)
    fixed[2].wait()
    table[own:] = mm(rows, w_recv[...]).astype(BF)
    wait_all(fixed[3:])

    def step(index, carry):
        here = pl.ds(pl.multiple_of(index * ROWS, ROWS), ROWS)
        hit = jnp.concatenate(
            [
                own_pick(
                    send[pl.ds(index * parts + part, 1), :],
                    recv[pl.ds(index * parts + part, 1), :],
                    own,
                )
                for part in range(parts)
            ],
            axis=0,
        )
        near = mm(hit, table[...]) + bias[...]
        for part in range(ratio):
            block_in(index * ratio + part).wait()
        value[here, :] = (near + mm(edges[here, :], w_edge[...])).astype(BF)
        for part in range(ratio):
            block_out(index * ratio + part).start()
        return carry

    lax.fori_loop(0, edges.shape[0] // ROWS, step, 0)
    for index in range(copies):
        block_out(index).wait()


def pipeline(stages):
    held = [None] * HALVES
    for wave in range(HALVES + len(stages) - 1):
        for index in range(HALVES):
            if 0 <= wave - index < len(stages):
                held[index] = stages[wave - index](index, held[index])
    total = held[0]
    for value in held[1:]:
        total = total + value
    return total


def main_kernel(shift, steps, *refs):
    take = iter(refs)
    received = [next(take) for _ in range(3)]
    coarse = next(take)
    sources = [next(take) for _ in range(FIXED)]
    block_sources = [next(take) for _ in range(3)]
    pair_out, first_out, second_out, far_out = [next(take) for _ in range(4)]
    new_nodes_out, d_node_out, new_edges_out, d_pre_out = [next(take) for _ in range(4)]
    targets = [next(take) for _ in range(FIXED)]
    pre_in, edges, edge_cot = block_targets = [next(take) for _ in range(3)]
    new_nodes, d_node, new_edges, d_pre = [next(take) for _ in range(4)]
    stack, rows2, table2, slope, unit, inverse, d_agg = [next(take) for _ in range(7)]
    load, store = next(take), next(take)
    far_lists, w_send, send, recv, w_edge_out, edge_out_bias, edge_gain, count = targets[:8]
    nodes, w_agg, w_node, node_bias, w_node_out, node_out_bias, node_cot, node_gain = targets[8:]
    own = nodes.shape[0]
    width = nodes.shape[1]
    far_width, peers = far_lists.shape
    near_width = first_out.shape[0]
    core, odd = place()
    near_rows = steps * near_width
    height = table2.shape[0]
    coarse_rows = coarse.shape[0] // peers
    half = edges.shape[0] // HALVES
    parts = half // LANES
    copies = edges.shape[0] // COPY
    fixed = copies_of(sources, targets, load)

    whole = copies_of(block_sources, block_targets, load.at[pl.ds(FIXED, 3)])
    edge_outs = copies_of((new_edges, d_pre), (new_edges_out, d_pre_out), store.at[pl.ds(2, 2)])
    node_outs = [
        pltpu.make_async_copy(new_nodes, new_nodes_out, store.at[0]),
        pltpu.make_async_copy(d_node, d_node_out, store.at[1]),
    ]
    start_all(fixed[:4])
    whole[0].start()
    start_all(fixed[4:])
    start_all(whole[1:])
    fixed[0].wait()
    far_ids = lax.broadcasted_iota(jnp.int32, (coarse.shape[0], peers), 0)
    far_base = lax.broadcasted_iota(jnp.int32, (coarse.shape[0], peers), 1) * coarse_rows
    far_hits = [
        ones_where(far_ids == far_base + far_lists[slot : slot + 1, :])
        for slot in range(far_width)
    ]
    rows2[...] = jnp.zeros(rows2.shape, BF)
    for index, ref in enumerate(received):
        stack[2 * index * near_width : 2 * (index + 1) * near_width] = ref[...]
    below = 4 - 2 * odd
    above = 2 + 2 * odd
    chosen = [
        jnp.where(core == 0, below + 1, odd),
        jnp.where(core == 0, 1 - odd, above + 1),
        below,
        above,
    ]
    for index, slot in enumerate(chosen):
        start = pl.multiple_of(slot * near_width, near_width)
        rows2[index * near_width : (index + 1) * near_width] = stack[pl.ds(start, near_width), :]
    for slot in range(far_width):
        start = near_rows + slot * peers
        rows2[start : start + peers] = mm_l(far_hits[slot], coarse[...]).astype(BF)
    fixed[1].wait()
    table2[...] = mm(rows2[...], w_send[...]).astype(BF)
    wait_all(fixed[2:8])

    def live_gain(block):
        return edge_gain[...] * jnp.where(count[...] > block, 1.0, 0.0)

    def picked(ref, index, part):
        here = index * parts + part
        return ref[here : here + 1, :]

    def remote_row(index, part):
        return remote_index(picked(send, index, part), own, near_rows, peers, shift)

    def pick_remote(index, _):
        hit = jnp.concatenate(
            [pick(remote_row(index, part), height) for part in range(parts)], axis=0
        )
        return mm(hit, table2[...])

    def activate(index, remote):
        if index == 0:
            whole[0].wait()
        hidden = []
        for low in range(0, half, CHUNK):
            here = slice(index * half + low, index * half + low + CHUNK)
            value = pre_in[here, :].astype(F32) + remote[low : low + CHUNK]
            part_hidden, part_slope = silu_parts(value)
            slope[here, :] = part_slope
            hidden.append(part_hidden.astype(BF))
        return jnp.concatenate(hidden, axis=0)

    def project(index, hidden):
        return mm(hidden, w_edge_out[...])

    def message_of(index, out):
        sent = []
        for low in range(0, half, CHUNK):
            here = slice(index * half + low, index * half + low + CHUNK)
            if low % BLOCK == 0:
                gain = live_gain((index * half + low) // BLOCK)
            part_unit, part_inverse = norm_parts(out[low : low + CHUNK] + edge_out_bias[...])
            unit[here, :] = part_unit
            inverse[here, :] = part_inverse
            sent.append((part_unit * gain).astype(BF))
        return jnp.concatenate(sent, axis=0)

    def gather_up(index, sent):
        hit = jnp.concatenate(
            [pick_t(picked(recv, index, part), own) for part in range(parts)], axis=1
        )
        return mm(hit, sent)

    total = pipeline([pick_remote, activate, project, message_of, gather_up])
    wait_all(fixed[8:])
    wait_all(whole[1:])
    rows = nodes[...]
    pre_node = mm(rows, w_node[...]) + mm(total.astype(BF), w_agg[...]) + node_bias[...]
    node_hidden, node_slope = silu_parts(pre_node)
    node_out = mm(node_hidden.astype(BF), w_node_out[...]) + node_out_bias[...]
    node_unit, node_inverse = norm_parts(node_out)
    new_nodes[...] = (rows.astype(F32) + node_gain[...] * node_unit).astype(BF)
    cot = node_cot[...].astype(F32)
    d_out = norm_back(cot * node_gain[...], node_unit, node_inverse).astype(BF)
    d_hidden = mm_t(d_out, w_node_out[...]).astype(BF).astype(F32)
    d_pre_node = (d_hidden * node_slope).astype(BF)
    d_agg[...] = jnp.zeros(d_agg.shape, BF)
    d_agg[:own] = mm_t(d_pre_node, w_agg[...]).astype(BF)
    d_node[...] = cot + mm_t(d_pre_node, w_node[...])
    for low in range(0, edges.shape[0], CHUNK):
        here = slice(low, low + CHUNK)
        if low % BLOCK == 0:
            gain = live_gain(low // BLOCK)
        new_edges[here, :] = (edges[here, :].astype(F32) + unit[here, :] * gain).astype(BF)
    start_all(node_outs)
    edge_outs[0].start()

    def pick_back(index, _):
        hit = jnp.concatenate(
            [pick(picked(recv, index, part), d_agg.shape[0]) for part in range(parts)], axis=0
        )
        return mm(hit, d_agg[...])

    def norm_grad(index, d_sent):
        outs = []
        for low in range(0, half, CHUNK):
            here = slice(index * half + low, index * half + low + CHUNK)
            if low % BLOCK == 0:
                gain = live_gain((index * half + low) // BLOCK)
            d_message = edge_cot[here, :].astype(F32) + d_sent[low : low + CHUNK]
            outs.append(norm_back(d_message * gain, unit[here, :], inverse[here, :]).astype(BF))
        return jnp.concatenate(outs, axis=0)

    def project_back(index, d_out):
        return mm_t(d_out, w_edge_out[...])

    def activate_back(index, d_hid):
        grads = []
        for low in range(0, half, CHUNK):
            here = slice(index * half + low, index * half + low + CHUNK)
            part = (d_hid[low : low + CHUNK] * slope[here, :]).astype(BF)
            d_pre[here, :] = part
            grads.append(part)
        return jnp.concatenate(grads, axis=0)

    def gather_back(index, grads):
        hit = jnp.concatenate(
            [pick_t(remote_row(index, part), height) for part in range(parts)], axis=1
        )
        return mm(hit, grads)

    sums2 = pipeline([pick_back, norm_grad, project_back, activate_back, gather_back])
    edge_outs[1].start()

    d_rows2 = mm_t(sums2.astype(BF), w_send[...])
    stack[: steps * near_width] = d_rows2[: steps * near_width].astype(BF)
    outgoing = [
        (pair_out, 0, 1 - core),
        (pair_out, 1, core),
        (first_out, 0, 3 - odd),
        (second_out, 0, 2 + odd),
    ]
    for ref, index, slot in outgoing:
        start = pl.multiple_of(slot * near_width, near_width)
        ref[index * near_width : (index + 1) * near_width] = stack[pl.ds(start, near_width), :]
    d_coarse = None
    for slot in range(far_width):
        start = near_rows + slot * peers
        term = mm(far_hits[slot], d_rows2[start : start + peers].astype(BF))
        d_coarse = term if d_coarse is None else d_coarse + term
    far_out[...] = d_coarse.astype(BF)
    wait_all(edge_outs)
    wait_all(node_outs)


def local_back_kernel(*refs):
    sources, block_sources = refs[:8], refs[8:10]
    edge_grad_out, node_sum, near_hit = refs[10:13]
    targets, block_targets = refs[13:21], refs[21:23]
    edge_grad, sums, load, store = refs[23:]
    send, recv, w_edge, w_send, w_recv, d_node, lists, coarse = targets
    d_pre, cot = block_targets
    own = d_node.shape[0]
    parts = ROWS // LANES
    copies = d_pre.shape[0] // COPY
    ratio = ROWS // COPY
    fixed = copies_of(sources, targets, load)

    def block_in(which, index):
        here = rows_of(index)
        return pltpu.make_async_copy(
            block_sources[which].at[here, :],
            block_targets[which].at[here, :],
            load.at[8 + which * copies + index],
        )

    def block_out(index):
        here = rows_of(index)
        return pltpu.make_async_copy(edge_grad.at[here, :], edge_grad_out.at[here, :], store.at[index])

    start_all(fixed[:3])
    for index in range(copies):
        block_in(0, index).start()
        block_in(1, index).start()
    start_all(fixed[3:])
    sums[...] = jnp.zeros(sums.shape, F32)
    wait_all(fixed[:3])

    def step(index, carry):
        here = pl.ds(pl.multiple_of(index * ROWS, ROWS), ROWS)
        hit = jnp.concatenate(
            [
                own_pick_t(
                    send[pl.ds(index * parts + part, 1), :],
                    recv[pl.ds(index * parts + part, 1), :],
                    own,
                )
                for part in range(parts)
            ],
            axis=1,
        )
        for part in range(ratio):
            block_in(0, index * ratio + part).wait()
            block_in(1, index * ratio + part).wait()
        grads = d_pre[here, :]
        value = cot[here, :].astype(F32) + mm_t(grads, w_edge[...])
        edge_grad[here, :] = value.astype(BF)
        for part in range(ratio):
            block_out(index * ratio + part).start()
        sums[...] += mm(hit, grads)
        return carry

    lax.fori_loop(0, d_pre.shape[0] // ROWS, step, 0)
    wait_all(fixed[3:])
    total = sums[...].astype(BF)
    node_sum[...] = d_node[...] + mm_t(total[:own], w_send[...]) + mm_t(total[own:], w_recv[...])
    width = lists.shape[1]
    ids = lax.broadcasted_iota(jnp.int32, (own, width), 0)
    core, odd = place()
    same = jnp.where(core == odd, 0, 2 * own)
    other = jnp.where(core == odd, 2 * own, 0)
    hits = [(core, 0), (2 + odd, 0), (odd, other), (3 - odd, 0), (1 - odd, same)]
    count = coarse.shape[1]
    far_slots = near_hit.shape[1] - 5 * width
    spread = ones_where(
        (lax.broadcasted_iota(jnp.int32, (count, far_slots), 1) & (count - 1))
        == lax.broadcasted_iota(jnp.int32, (count, far_slots), 0)
    )
    coarse_hit = ones_where(lax.broadcasted_iota(jnp.int32, (own, count), 0) == coarse[...])
    near_hit[:, : 5 * width] = jnp.concatenate(
        [ones_where(ids == lists[pl.ds(index, 1), :] + away) for index, away in hits], axis=1
    )
    near_hit[:, 5 * width :] = mm(coarse_hit, spread).astype(BF)
    for index in range(copies):
        block_out(index).wait()


def combine_kernel(node_sum, hit, far, pair, first, second, out):
    width = pair.shape[0] // 2
    rows = jnp.concatenate([pair[:width], first[...], second[...], far[...]], axis=0)
    out[...] = (node_sum[...] + mm(hit[...], rows)).astype(BF)


def vmem(count):
    return [pl.BlockSpec(memory_space=pltpu.VMEM) for _ in range(count)]


def hbm(count):
    return [pl.BlockSpec(memory_space=pltpu.HBM) for _ in range(count)]


def local(
    nodes,
    edges,
    node_cot,
    edge_cot,
    w_edge,
    w_send,
    w_recv,
    edge_bias,
    w_edge_out,
    edge_out_bias,
    edge_gain,
    w_node,
    w_agg,
    node_bias,
    w_node_out,
    node_out_bias,
    node_gain,
    send_slots,
    recv_slots,
    neighbour_send_lists,
    coarse_rows,
    far_lists,
    block_count,
):
    own, width = nodes.shape
    hidden = w_edge.shape[1]
    edge_rows = edges.shape[0]
    peers = lax.axis_size("patch")
    steps, near_width = neighbour_send_lists.shape
    coarse_count = coarse_rows.shape[0]
    far_width = far_lists.shape[2]
    shift = far_width.bit_length() - 1
    if steps != 4 or coarse_count & (coarse_count - 1) or (5 * near_width) % 64 or peers % 4 or far_width != 1 << shift or own % 64 or edge_rows % ROWS or edge_rows % (HALVES * BLOCK) or hidden != width:
        raise ValueError("unsupported sizes")
    slots = steps * near_width + peers * far_width
    height = -(-slots // LANES) * LANES
    own_pad = -(-own // LANES) * LANES
    send = send_slots.reshape(-1, LANES)
    recv = recv_slots.reshape(-1, LANES)
    blocks = edge_rows // ROWS
    copies = edge_rows // COPY
    row = lambda value: value.reshape(1, -1)
    shape = jax.ShapeDtypeStruct

    small = lambda: pltpu.VMEM((1, width), F32)
    square = lambda: pltpu.VMEM((width, hidden), BF)
    index_rows = lambda: pltpu.VMEM((edge_rows // LANES, LANES), jnp.int32)
    edge_like = lambda: pltpu.VMEM((edge_rows, width), BF)
    node_like = lambda: pltpu.VMEM((own, width), BF)
    here = lambda value: pltpu.with_memory_space_constraint(value, pltpu.VMEM)

    near_like = pltpu.VMEM((near_width, width), BF)
    pair_like = pltpu.VMEM((2 * near_width, width), BF)

    def exchanged(pair, first, second, rows, relay):
        pair = here(swapped(pair, "patch", 1, 0))
        rows = lax.all_to_all(rows, "patch", split_axis=0, concat_axis=0, tiled=True)
        first, second = pl.pallas_call(
            lambda *refs: join_kernel(relay, *refs),
            out_shape=[pair_like] * 2,
            in_specs=vmem(3),
            out_specs=vmem(2),
            name="join",
        )(pair, here(first), here(second))
        first = here(swapped(first, "patch", 2, 0))
        second = here(swapped(second, "patch", 2, 2))
        return pair, first, second, rows

    packed = pl.pallas_call(
        pack_kernel,
        out_shape=[pair_like, near_like, near_like, shape((peers, coarse_count, width), BF)],
        in_specs=vmem(3),
        out_specs=vmem(4),
        name="pack",
    )(nodes, neighbour_send_lists, row(coarse_rows))
    *near, coarse = exchanged(*packed, (0, 1))

    pre_local = pl.pallas_call(
        local_kernel,
        out_shape=shape((edge_rows, hidden), BF),
        in_specs=hbm(8),
        out_specs=hbm(1)[0],
        scratch_shapes=[
            node_like(),
            square(),
            square(),
            index_rows(),
            index_rows(),
            square(),
            small(),
            edge_like(),
            pltpu.VMEM((2 * own, hidden), BF),
            edge_like(),
            pltpu.SemaphoreType.DMA((7 + copies,)),
            pltpu.SemaphoreType.DMA((copies,)),
        ],
        cost_estimate=pl.CostEstimate(
            flops=2 * edge_rows * width * hidden * 3, transcendentals=0, bytes_accessed=6 << 20
        ),
        name="local_ahead",
    )(nodes, w_send, w_recv, send, recv, w_edge, row(edge_bias), edges)

    outs = pl.pallas_call(
        lambda *refs: main_kernel(shift, steps, *refs),
        out_shape=[
            pair_like,
            near_like,
            near_like,
            shape((peers * coarse_count, width), BF),
            shape((own, width), BF),
            shape((own, width), F32),
            shape((edge_rows, width), BF),
            shape((edge_rows, hidden), BF),
        ],
        in_specs=vmem(4) + hbm(FIXED + 3),
        out_specs=vmem(4) + hbm(4),
        scratch_shapes=[
            pltpu.VMEM((far_width, peers), jnp.int32),
            square(),
            index_rows(),
            index_rows(),
            square(),
            small(),
            small(),
            pltpu.VMEM((1, 1), jnp.int32),
            node_like(),
            square(),
            square(),
            small(),
            square(),
            small(),
            node_like(),
            small(),
            edge_like(),
            edge_like(),
            edge_like(),
            node_like(),
            pltpu.VMEM((own, width), F32),
            edge_like(),
            edge_like(),
            pltpu.VMEM((6 * near_width, width), BF),
            pltpu.VMEM((height, width), BF),
            pltpu.VMEM((height, hidden), BF),
            pltpu.VMEM((edge_rows, hidden), F32),
            pltpu.VMEM((edge_rows, width), F32),
            pltpu.VMEM((edge_rows, 1), F32),
            pltpu.VMEM((own_pad, width), BF),
            pltpu.SemaphoreType.DMA((FIXED + 3,)),
            pltpu.SemaphoreType.DMA((4,)),
        ],
        cost_estimate=pl.CostEstimate(
            flops=2 * edge_rows * width * hidden * 8, transcendentals=0, bytes_accessed=16 << 20
        ),
        name="main",
    )(
        *near,
        here(coarse.reshape(-1, width)),
        far_lists[0].T,
        w_send,
        send,
        recv,
        w_edge_out,
        row(edge_out_bias),
        row(edge_gain),
        block_count.reshape(1, 1),
        nodes,
        w_agg,
        w_node,
        row(node_bias),
        w_node_out,
        row(node_out_bias),
        node_cot,
        row(node_gain),
        pre_local,
        edges,
        edge_cot,
    )
    new_nodes, d_node, new_edges, d_pre = outs[4:]
    *returned, far_back = exchanged(
        *outs[:3], outs[3].reshape(peers, coarse_count, width), (1, 1)
    )

    edge_grad, node_sum, near_hit = pl.pallas_call(
        local_back_kernel,
        out_shape=[
            shape((edge_rows, width), BF),
            pltpu.VMEM((own, width), F32),
            pltpu.VMEM((own, 5 * near_width + peers * coarse_count), BF),
        ],
        in_specs=hbm(10),
        out_specs=hbm(1) + vmem(2),
        scratch_shapes=[
            index_rows(),
            index_rows(),
            square(),
            square(),
            square(),
            pltpu.VMEM((own, width), F32),
            pltpu.VMEM((steps, near_width), jnp.int32),
            pltpu.VMEM((1, coarse_count), jnp.int32),
            edge_like(),
            edge_like(),
            edge_like(),
            pltpu.VMEM((2 * own, hidden), F32),
            pltpu.SemaphoreType.DMA((8 + 2 * copies,)),
            pltpu.SemaphoreType.DMA((copies,)),
        ],
        cost_estimate=pl.CostEstimate(
            flops=2 * edge_rows * width * hidden * 3, transcendentals=0, bytes_accessed=6 << 20
        ),
        name="local_back",
    )(
        send,
        recv,
        w_edge,
        w_send,
        w_recv,
        d_node,
        neighbour_send_lists,
        row(coarse_rows),
        d_pre,
        edge_cot,
    )

    node_grad = pl.pallas_call(
        combine_kernel,
        out_shape=shape((own, width), BF),
        in_specs=vmem(6),
        out_specs=vmem(1)[0],
        name="combine",
    )(here(node_sum), here(near_hit), here(far_back.reshape(-1, width)), *returned)
    return new_nodes, new_edges, node_grad, edge_grad


def solution(mesh):
    rows = P(("groups", "patch"), None)
    placed = (
        (rows,) * 4
        + (P(),) * 13
        + (
            P("patch"),
            P("patch"),
            P("patch", None),
            P("patch"),
            P("patch", None, None),
            P("patch"),
        )
    )
    return jax.shard_map(
        local,
        mesh=mesh,
        in_specs=placed,
        out_specs=(rows,) * 4,
        check_vma=False,
    )
```

```python
import jax
import jax.numpy as jnp
from jax import lax
from jax.experimental import pallas as pl
from jax.experimental.pallas import tpu as pltpu
from jax.sharding import PartitionSpec as P

BLOCK = 128
LANES = 128
ROWS = 512
HALVES = 2
COPY = 256
CHUNK = 16
FIXED = 13
EPS = 1e-05
BF = jnp.bfloat16
F32 = jnp.float32


def swapped(value, axis, bit, shift):
    count = lax.axis_size(axis)
    pairs = [(source, (((source + shift) ^ bit) - shift) % count) for source in range(count)]
    return lax.ppermute(value, axis, pairs)


def mm(a, b):
    return lax.dot_general(a, b, (((1,), (0,)), ((), ())), preferred_element_type=F32)


def mm_t(a, b):
    return lax.dot_general(a, b, (((1,), (1,)), ((), ())), preferred_element_type=F32)


def mm_l(a, b):
    return lax.dot_general(a, b, (((0,), (0,)), ((), ())), preferred_element_type=F32)


def ones_where(mask):
    return jnp.where(mask, 1.0, 0.0).astype(BF)


def as_columns(row):
    return jnp.broadcast_to(row.astype(F32), (LANES, LANES)).T.astype(jnp.int32)


def lane_ids(tile):
    return lax.broadcasted_iota(jnp.int32, (LANES, LANES), 1) + tile * LANES


def own_pick(send, recv, own):
    sender = as_columns(jnp.where(send < own, send, -1))
    receiver = as_columns(recv + own)
    tiles = []
    for tile in range(2 * own // LANES):
        ids = lane_ids(tile)
        if (tile + 1) * LANES <= own:
            hit = sender == ids
        elif tile * LANES >= own:
            hit = receiver == ids
        else:
            hit = (sender == ids) | (receiver == ids)
        tiles.append(ones_where(hit))
    return jnp.concatenate(tiles, axis=1)


def own_pick_t(send, recv, own):
    sender = jnp.where(send < own, send, -1)
    ids = lax.broadcasted_iota(jnp.int32, (own, LANES), 0)
    return jnp.concatenate([ones_where(ids == sender), ones_where(ids == recv)], axis=0)


def remote_index(send, own, near, peers, shift):
    far = send - (own + near)
    far_index = near + (far & ((1 << shift) - 1)) * peers + (far >> shift)
    return jnp.where(send < own + near, send - own, far_index)


def pick(row, width):
    column = as_columns(row)
    return jnp.concatenate(
        [ones_where(column == lane_ids(tile)) for tile in range(width // LANES)], axis=1
    )


def pick_t(row, height):
    return ones_where(lax.broadcasted_iota(jnp.int32, (height, LANES), 0) == row)


def silu_parts(value):
    gate = 0.5 * jnp.tanh(0.5 * value) + 0.5
    hidden = value * gate
    slope = gate * (1.0 + value - hidden)
    return hidden, slope


def norm_parts(value):
    center = value - jnp.mean(value, axis=-1, keepdims=True)
    inverse = lax.rsqrt(jnp.mean(center * center, axis=-1, keepdims=True) + EPS)
    return center * inverse, inverse


def norm_back(grad, unit, inverse):
    first = jnp.mean(grad, axis=-1, keepdims=True)
    second = jnp.mean(grad * unit, axis=-1, keepdims=True)
    return inverse * (grad - first - unit * second)


def copies_of(sources, targets, sems):
    return [
        pltpu.make_async_copy(source, target, sems.at[index])
        for index, (source, target) in enumerate(zip(sources, targets))
    ]


def start_all(copies):
    for copy in copies:
        copy.start()


def wait_all(copies):
    for copy in copies:
        copy.wait()


def rows_of(index):
    return pl.ds(pl.multiple_of(index * COPY, COPY), COPY)


def place():
    index = lax.axis_index("patch")
    return index & 1, (index >> 1) & 1


def pack_kernel(nodes, lists, coarse, pair_out, first_out, second_out, out, chosen, sems):
    rows = nodes[...]
    own = rows.shape[0]
    width = lists.shape[1]
    _, odd = place()
    ids = lax.broadcasted_iota(jnp.int32, (own, width), 0)

    def picked(index):
        return mm_l(ones_where(ids == lists[pl.ds(index, 1), :]), rows).astype(BF)

    count = coarse.shape[1]
    hit = ones_where(lax.broadcasted_iota(jnp.int32, (own, count), 0) == coarse[...])
    chosen[...] = mm_l(hit, rows).astype(BF)

    def copy_to(index):
        return pltpu.make_async_copy(chosen, out.at[index], sems.at[index])

    def put(index, carry):
        copy_to(index).start()
        return carry

    def done(index, carry):
        copy_to(index).wait()
        return carry

    lax.fori_loop(0, out.shape[0], put, 0)
    pair_out[:width] = picked(odd)
    pair_out[width:] = picked(1 - odd)
    first_out[...] = picked(2 + odd)
    second_out[...] = picked(3 - odd)
    lax.fori_loop(0, out.shape[0], done, 0)


def join_kernel(relay, pair, first, second, first_out, second_out):
    width = first.shape[0]
    first_out[:width] = first[...]
    first_out[width:] = pair[relay[0] * width : (relay[0] + 1) * width]
    second_out[:width] = second[...]
    second_out[width:] = pair[relay[1] * width : (relay[1] + 1) * width]


def local_kernel(*refs):
    sources, edges_in, out = refs[:7], refs[7], refs[8]
    w_send, send, recv, nodes, w_recv, w_edge, bias, edges, table, value, load, store = refs[9:]
    targets = (nodes, w_send, w_recv, send, recv, w_edge, bias)
    own = nodes.shape[0]
    parts = ROWS // LANES
    copies = edges.shape[0] // COPY
    ratio = ROWS // COPY
    fixed = copies_of(sources, targets, load)

    def block_in(index):
        here = rows_of(index)
        return pltpu.make_async_copy(edges_in.at[here, :], edges.at[here, :], load.at[7 + index])

    def block_out(index):
        here = rows_of(index)
        return pltpu.make_async_copy(value.at[here, :], out.at[here, :], store.at[index])

    start_all(fixed)
    for index in range(copies):
        block_in(index).start()
    wait_all(fixed[:2])
    rows = nodes[...]
    table[:own] = mm(rows, w_send[...]).astype(BF)
    fixed[2].wait()
    table[own:] = mm(rows, w_recv[...]).astype(BF)
    wait_all(fixed[3:])

    def step(index, carry):
        here = pl.ds(pl.multiple_of(index * ROWS, ROWS), ROWS)
        hit = jnp.concatenate(
            [
                own_pick(
                    send[pl.ds(index * parts + part, 1), :],
                    recv[pl.ds(index * parts + part, 1), :],
                    own,
                )
                for part in range(parts)
            ],
            axis=0,
        )
        near = mm(hit, table[...]) + bias[...]
        for part in range(ratio):
            block_in(index * ratio + part).wait()
        value[here, :] = (near + mm(edges[here, :], w_edge[...])).astype(BF)
        for part in range(ratio):
            block_out(index * ratio + part).start()
        return carry

    lax.fori_loop(0, edges.shape[0] // ROWS, step, 0)
    for index in range(copies):
        block_out(index).wait()


def pipeline(stages):
    held = [None] * HALVES
    for wave in range(HALVES + len(stages) - 1):
        for index in range(HALVES):
            if 0 <= wave - index < len(stages):
                held[index] = stages[wave - index](index, held[index])
    total = held[0]
    for value in held[1:]:
        total = total + value
    return total


def main_kernel(shift, steps, *refs):
    take = iter(refs)
    received = [next(take) for _ in range(3)]
    coarse, w_send, send, recv = [next(take) for _ in range(4)]
    sources = [next(take) for _ in range(FIXED)]
    block_sources = [next(take) for _ in range(3)]
    pair_out, first_out, second_out, far_out = [next(take) for _ in range(4)]
    new_nodes_out, d_node_out, new_edges_out, d_pre_out = [next(take) for _ in range(4)]
    targets = [next(take) for _ in range(FIXED)]
    pre_in, edges, edge_cot = block_targets = [next(take) for _ in range(3)]
    new_nodes, d_node, new_edges, d_pre = [next(take) for _ in range(4)]
    stack, rows2, table2, slope, unit, inverse, d_agg, far_rows = [next(take) for _ in range(8)]
    load, store = next(take), next(take)
    far_lists, w_edge_out, edge_out_bias, edge_gain, count = targets[:5]
    nodes, w_agg, w_node, node_bias, w_node_out, node_out_bias, node_cot, node_gain = targets[5:]
    own = nodes.shape[0]
    width = nodes.shape[1]
    far_width, peers = far_lists.shape
    near_width = first_out.shape[0]
    core, odd = place()
    near_rows = steps * near_width
    height = table2.shape[0]
    coarse_rows = coarse.shape[0] // peers
    half = edges.shape[0] // HALVES
    parts = half // LANES
    copies = edges.shape[0] // COPY
    fixed = copies_of(sources, targets, load)

    whole = copies_of(block_sources, block_targets, load.at[pl.ds(FIXED, 3)])
    edge_outs = copies_of((new_edges, d_pre), (new_edges_out, d_pre_out), store.at[pl.ds(2, 2)])
    node_outs = [
        pltpu.make_async_copy(new_nodes, new_nodes_out, store.at[0]),
        pltpu.make_async_copy(d_node, d_node_out, store.at[1]),
    ]
    fixed[0].start()
    whole[0].start()
    start_all(fixed[1:])
    start_all(whole[1:])
    fixed[0].wait()
    far_ids = lax.broadcasted_iota(jnp.int32, (coarse.shape[0], peers), 0)
    far_base = lax.broadcasted_iota(jnp.int32, (coarse.shape[0], peers), 1) * coarse_rows
    far_hits = [
        ones_where(far_ids == far_base + far_lists[slot : slot + 1, :])
        for slot in range(far_width)
    ]
    rows2[...] = jnp.zeros(rows2.shape, BF)
    for index, ref in enumerate(received):
        stack[2 * index * near_width : 2 * (index + 1) * near_width] = ref[...]
    below = 4 - 2 * odd
    above = 2 + 2 * odd
    chosen = [
        jnp.where(core == 0, below + 1, odd),
        jnp.where(core == 0, 1 - odd, above + 1),
        below,
        above,
    ]
    for index, slot in enumerate(chosen):
        start = pl.multiple_of(slot * near_width, near_width)
        rows2[index * near_width : (index + 1) * near_width] = stack[pl.ds(start, near_width), :]
    for slot in range(far_width):
        start = near_rows + slot * peers
        rows2[start : start + peers] = mm_l(far_hits[slot], coarse[...]).astype(BF)
    table2[...] = mm(rows2[...], w_send[...]).astype(BF)
    def live_gain(block):
        return edge_gain[...] * jnp.where(count[...] > block, 1.0, 0.0)

    def picked(ref, index, part):
        here = index * parts + part
        return ref[here : here + 1, :]

    def remote_row(index, part):
        return remote_index(picked(send, index, part), own, near_rows, peers, shift)

    def pick_remote(index, _):
        hit = jnp.concatenate(
            [pick(remote_row(index, part), height) for part in range(parts)], axis=0
        )
        return mm(hit, table2[...])

    def activate(index, remote):
        if index == 0:
            whole[0].wait()
            wait_all(fixed[1:5])
        hidden = []
        for low in range(0, half, CHUNK):
            here = slice(index * half + low, index * half + low + CHUNK)
            value = pre_in[here, :].astype(F32) + remote[low : low + CHUNK]
            part_hidden, part_slope = silu_parts(value)
            slope[here, :] = part_slope
            hidden.append(part_hidden.astype(BF))
        return jnp.concatenate(hidden, axis=0)

    def project(index, hidden):
        return mm(hidden, w_edge_out[...])

    def message_of(index, out):
        sent = []
        for low in range(0, half, CHUNK):
            here = slice(index * half + low, index * half + low + CHUNK)
            if low % BLOCK == 0:
                gain = live_gain((index * half + low) // BLOCK)
            part_unit, part_inverse = norm_parts(out[low : low + CHUNK] + edge_out_bias[...])
            unit[here, :] = part_unit
            inverse[here, :] = part_inverse
            sent.append((part_unit * gain).astype(BF))
        return jnp.concatenate(sent, axis=0)

    def gather_up(index, sent):
        hit = jnp.concatenate(
            [pick_t(picked(recv, index, part), own) for part in range(parts)], axis=1
        )
        return mm(hit, sent)

    total = pipeline([pick_remote, activate, project, message_of, gather_up])
    wait_all(fixed[5:])
    wait_all(whole[1:])
    rows = nodes[...]
    pre_node = mm(rows, w_node[...]) + mm(total.astype(BF), w_agg[...]) + node_bias[...]
    node_hidden, node_slope = silu_parts(pre_node)
    node_out = mm(node_hidden.astype(BF), w_node_out[...]) + node_out_bias[...]
    node_unit, node_inverse = norm_parts(node_out)
    new_nodes[...] = (rows.astype(F32) + node_gain[...] * node_unit).astype(BF)
    cot = node_cot[...].astype(F32)
    d_out = norm_back(cot * node_gain[...], node_unit, node_inverse).astype(BF)
    d_hidden = mm_t(d_out, w_node_out[...]).astype(BF).astype(F32)
    d_pre_node = (d_hidden * node_slope).astype(BF)
    d_agg[...] = jnp.zeros(d_agg.shape, BF)
    d_agg[:own] = mm_t(d_pre_node, w_agg[...]).astype(BF)
    d_node[...] = cot + mm_t(d_pre_node, w_node[...])
    for low in range(0, edges.shape[0], CHUNK):
        here = slice(low, low + CHUNK)
        if low % BLOCK == 0:
            gain = live_gain(low // BLOCK)
        new_edges[here, :] = (edges[here, :].astype(F32) + unit[here, :] * gain).astype(BF)
    start_all(node_outs)
    edge_outs[0].start()

    def pick_back(index, _):
        hit = jnp.concatenate(
            [pick(picked(recv, index, part), d_agg.shape[0]) for part in range(parts)], axis=0
        )
        return mm(hit, d_agg[...])

    def norm_grad(index, d_sent):
        outs = []
        for low in range(0, half, CHUNK):
            here = slice(index * half + low, index * half + low + CHUNK)
            if low % BLOCK == 0:
                gain = live_gain((index * half + low) // BLOCK)
            d_message = edge_cot[here, :].astype(F32) + d_sent[low : low + CHUNK]
            outs.append(norm_back(d_message * gain, unit[here, :], inverse[here, :]).astype(BF))
        return jnp.concatenate(outs, axis=0)

    def project_back(index, d_out):
        return mm_t(d_out, w_edge_out[...])

    def activate_back(index, d_hid):
        grads = []
        for low in range(0, half, CHUNK):
            here = slice(index * half + low, index * half + low + CHUNK)
            part = (d_hid[low : low + CHUNK] * slope[here, :]).astype(BF)
            d_pre[here, :] = part
            grads.append(part)
        return jnp.concatenate(grads, axis=0)

    def gather_back(index, grads):
        hit = jnp.concatenate(
            [pick_t(remote_row(index, part), height) for part in range(parts)], axis=1
        )
        return mm(hit, grads)

    sums2 = pipeline([pick_back, norm_grad, project_back, activate_back, gather_back])
    edge_outs[1].start()

    sums2 = sums2.astype(BF)
    d_far = mm_t(sums2[near_rows:], w_send[...])
    d_coarse = None
    for slot in range(far_width):
        term = mm(far_hits[slot], d_far[slot * peers : (slot + 1) * peers].astype(BF))
        d_coarse = term if d_coarse is None else d_coarse + term
    far_rows[...] = d_coarse.astype(BF)
    far_copy = pltpu.make_async_copy(far_rows, far_out, store.at[4])
    far_copy.start()
    stack[: steps * near_width] = mm_t(sums2[:near_rows], w_send[...]).astype(BF)
    outgoing = [
        (pair_out, 0, 1 - core),
        (pair_out, 1, core),
        (first_out, 0, 3 - odd),
        (second_out, 0, 2 + odd),
    ]
    for ref, index, slot in outgoing:
        start = pl.multiple_of(slot * near_width, near_width)
        ref[index * near_width : (index + 1) * near_width] = stack[pl.ds(start, near_width), :]
    far_copy.wait()
    wait_all(edge_outs)
    wait_all(node_outs)


def local_back_kernel(*refs):
    sources, block_sources = refs[:8], refs[8:10]
    edge_grad_out, node_sum, near_hit = refs[10:13]
    targets, block_targets = refs[13:21], refs[21:23]
    edge_grad, sums, load, store = refs[23:]
    send, recv, w_edge, w_send, w_recv, d_node, lists, coarse = targets
    d_pre, cot = block_targets
    own = d_node.shape[0]
    parts = ROWS // LANES
    copies = d_pre.shape[0] // COPY
    ratio = ROWS // COPY
    fixed = copies_of(sources, targets, load)

    def block_in(which, index):
        here = rows_of(index)
        return pltpu.make_async_copy(
            block_sources[which].at[here, :],
            block_targets[which].at[here, :],
            load.at[8 + which * copies + index],
        )

    def block_out(index):
        here = rows_of(index)
        return pltpu.make_async_copy(edge_grad.at[here, :], edge_grad_out.at[here, :], store.at[index])

    start_all(fixed[:3])
    for index in range(copies):
        block_in(0, index).start()
        block_in(1, index).start()
    start_all(fixed[3:])
    sums[...] = jnp.zeros(sums.shape, F32)
    wait_all(fixed[:3])

    def step(index, carry):
        here = pl.ds(pl.multiple_of(index * ROWS, ROWS), ROWS)
        hit = jnp.concatenate(
            [
                own_pick_t(
                    send[pl.ds(index * parts + part, 1), :],
                    recv[pl.ds(index * parts + part, 1), :],
                    own,
                )
                for part in range(parts)
            ],
            axis=1,
        )
        for part in range(ratio):
            block_in(0, index * ratio + part).wait()
            block_in(1, index * ratio + part).wait()
        grads = d_pre[here, :]
        value = cot[here, :].astype(F32) + mm_t(grads, w_edge[...])
        edge_grad[here, :] = value.astype(BF)
        for part in range(ratio):
            block_out(index * ratio + part).start()
        sums[...] += mm(hit, grads)
        return carry

    lax.fori_loop(0, d_pre.shape[0] // ROWS, step, 0)
    wait_all(fixed[3:])
    total = sums[...].astype(BF)
    node_sum[...] = d_node[...] + mm_t(total[:own], w_send[...]) + mm_t(total[own:], w_recv[...])
    width = lists.shape[1]
    ids = lax.broadcasted_iota(jnp.int32, (own, width), 0)
    core, odd = place()
    same = jnp.where(core == odd, 0, 2 * own)
    other = jnp.where(core == odd, 2 * own, 0)
    hits = [(core, 0), (2 + odd, 0), (odd, other), (3 - odd, 0), (1 - odd, same)]
    count = coarse.shape[1]
    far_slots = near_hit.shape[1] - 5 * width
    spread = ones_where(
        (lax.broadcasted_iota(jnp.int32, (count, far_slots), 1) & (count - 1))
        == lax.broadcasted_iota(jnp.int32, (count, far_slots), 0)
    )
    coarse_hit = ones_where(lax.broadcasted_iota(jnp.int32, (own, count), 0) == coarse[...])
    near_hit[:, : 5 * width] = jnp.concatenate(
        [ones_where(ids == lists[pl.ds(index, 1), :] + away) for index, away in hits], axis=1
    )
    near_hit[:, 5 * width :] = mm(coarse_hit, spread).astype(BF)
    for index in range(copies):
        block_out(index).wait()


def combine_kernel(node_sum, hit, far, pair, first, second, out):
    width = pair.shape[0] // 2
    rows = jnp.concatenate([pair[:width], first[...], second[...], far[...]], axis=0)
    out[...] = (node_sum[...] + mm(hit[...], rows)).astype(BF)


def vmem(count):
    return [pl.BlockSpec(memory_space=pltpu.VMEM) for _ in range(count)]


def hbm(count):
    return [pl.BlockSpec(memory_space=pltpu.HBM) for _ in range(count)]


def local(
    nodes,
    edges,
    node_cot,
    edge_cot,
    w_edge,
    w_send,
    w_recv,
    edge_bias,
    w_edge_out,
    edge_out_bias,
    edge_gain,
    w_node,
    w_agg,
    node_bias,
    w_node_out,
    node_out_bias,
    node_gain,
    send_slots,
    recv_slots,
    neighbour_send_lists,
    coarse_rows,
    far_lists,
    block_count,
):
    own, width = nodes.shape
    hidden = w_edge.shape[1]
    edge_rows = edges.shape[0]
    peers = lax.axis_size("patch")
    steps, near_width = neighbour_send_lists.shape
    coarse_count = coarse_rows.shape[0]
    far_width = far_lists.shape[2]
    shift = far_width.bit_length() - 1
    if steps != 4 or coarse_count & (coarse_count - 1) or (5 * near_width) % 64 or peers % 4 or far_width != 1 << shift or own % 64 or edge_rows % ROWS or edge_rows % (HALVES * BLOCK) or hidden != width:
        raise ValueError("unsupported sizes")
    slots = steps * near_width + peers * far_width
    height = -(-slots // LANES) * LANES
    own_pad = -(-own // LANES) * LANES
    send = send_slots.reshape(-1, LANES)
    recv = recv_slots.reshape(-1, LANES)
    blocks = edge_rows // ROWS
    copies = edge_rows // COPY
    row = lambda value: value.reshape(1, -1)
    shape = jax.ShapeDtypeStruct

    small = lambda: pltpu.VMEM((1, width), F32)
    square = lambda: pltpu.VMEM((width, hidden), BF)
    index_rows = lambda: pltpu.VMEM((edge_rows // LANES, LANES), jnp.int32)
    edge_like = lambda: pltpu.VMEM((edge_rows, width), BF)
    node_like = lambda: pltpu.VMEM((own, width), BF)
    here = lambda value: pltpu.with_memory_space_constraint(value, pltpu.VMEM)

    near_like = pltpu.VMEM((near_width, width), BF)
    pair_like = pltpu.VMEM((2 * near_width, width), BF)

    def exchanged(pair, first, second, rows, relay):
        pair = here(swapped(pair, "patch", 1, 0))
        rows = lax.all_to_all(rows, "patch", split_axis=0, concat_axis=0, tiled=True)
        first, second = pl.pallas_call(
            lambda *refs: join_kernel(relay, *refs),
            out_shape=[pair_like] * 2,
            in_specs=vmem(3),
            out_specs=vmem(2),
            name="join",
        )(pair, here(first), here(second))
        first = here(swapped(first, "patch", 2, 0))
        second = here(swapped(second, "patch", 2, 2))
        return pair, first, second, rows

    packed = pl.pallas_call(
        pack_kernel,
        out_shape=[pair_like, near_like, near_like, shape((peers, coarse_count, width), BF)],
        in_specs=vmem(3),
        out_specs=vmem(3) + hbm(1),
        scratch_shapes=[
            pltpu.VMEM((coarse_count, width), BF),
            pltpu.SemaphoreType.DMA((peers,)),
        ],
        name="pack",
    )(nodes, neighbour_send_lists, row(coarse_rows))
    *near, coarse = exchanged(*packed, (0, 1))

    pre_local, *kept = pl.pallas_call(
        local_kernel,
        out_shape=[shape((edge_rows, hidden), BF), square(), index_rows(), index_rows()],
        in_specs=hbm(8),
        out_specs=hbm(1) + vmem(3),
        scratch_shapes=[
            node_like(),
            square(),
            square(),
            small(),
            edge_like(),
            pltpu.VMEM((2 * own, hidden), BF),
            edge_like(),
            pltpu.SemaphoreType.DMA((7 + copies,)),
            pltpu.SemaphoreType.DMA((copies,)),
        ],
        cost_estimate=pl.CostEstimate(
            flops=2 * edge_rows * width * hidden * 3, transcendentals=0, bytes_accessed=6 << 20
        ),
        name="local_ahead",
    )(nodes, w_send, w_recv, send, recv, w_edge, row(edge_bias), edges)

    outs = pl.pallas_call(
        lambda *refs: main_kernel(shift, steps, *refs),
        out_shape=[
            pair_like,
            near_like,
            near_like,
            shape((peers * coarse_count, width), BF),
            shape((own, width), BF),
            shape((own, width), F32),
            shape((edge_rows, width), BF),
            shape((edge_rows, hidden), BF),
        ],
        in_specs=vmem(7) + hbm(FIXED + 3),
        out_specs=vmem(3) + hbm(5),
        scratch_shapes=[
            pltpu.VMEM((far_width, peers), jnp.int32),
            square(),
            small(),
            small(),
            pltpu.VMEM((1, 1), jnp.int32),
            node_like(),
            square(),
            square(),
            small(),
            square(),
            small(),
            node_like(),
            small(),
            edge_like(),
            edge_like(),
            edge_like(),
            node_like(),
            pltpu.VMEM((own, width), F32),
            edge_like(),
            edge_like(),
            pltpu.VMEM((6 * near_width, width), BF),
            pltpu.VMEM((height, width), BF),
            pltpu.VMEM((height, hidden), BF),
            pltpu.VMEM((edge_rows, hidden), F32),
            pltpu.VMEM((edge_rows, width), F32),
            pltpu.VMEM((edge_rows, 1), F32),
            pltpu.VMEM((own_pad, width), BF),
            pltpu.VMEM((peers * coarse_count, width), BF),
            pltpu.SemaphoreType.DMA((FIXED + 3,)),
            pltpu.SemaphoreType.DMA((5,)),
        ],
        cost_estimate=pl.CostEstimate(
            flops=2 * edge_rows * width * hidden * 8, transcendentals=0, bytes_accessed=16 << 20
        ),
        name="main",
    )(
        *near,
        here(coarse.reshape(-1, width)),
        *[here(value) for value in kept],
        far_lists[0].T,
        w_edge_out,
        row(edge_out_bias),
        row(edge_gain),
        block_count.reshape(1, 1),
        nodes,
        w_agg,
        w_node,
        row(node_bias),
        w_node_out,
        row(node_out_bias),
        node_cot,
        row(node_gain),
        pre_local,
        edges,
        edge_cot,
    )
    new_nodes, d_node, new_edges, d_pre = outs[4:]
    *returned, far_back = exchanged(
        *outs[:3], outs[3].reshape(peers, coarse_count, width), (1, 1)
    )

    edge_grad, node_sum, near_hit = pl.pallas_call(
        local_back_kernel,
        out_shape=[
            shape((edge_rows, width), BF),
            pltpu.VMEM((own, width), F32),
            pltpu.VMEM((own, 5 * near_width + peers * coarse_count), BF),
        ],
        in_specs=hbm(10),
        out_specs=hbm(1) + vmem(2),
        scratch_shapes=[
            index_rows(),
            index_rows(),
            square(),
            square(),
            square(),
            pltpu.VMEM((own, width), F32),
            pltpu.VMEM((steps, near_width), jnp.int32),
            pltpu.VMEM((1, coarse_count), jnp.int32),
            edge_like(),
            edge_like(),
            edge_like(),
            pltpu.VMEM((2 * own, hidden), F32),
            pltpu.SemaphoreType.DMA((8 + 2 * copies,)),
            pltpu.SemaphoreType.DMA((copies,)),
        ],
        cost_estimate=pl.CostEstimate(
            flops=2 * edge_rows * width * hidden * 3, transcendentals=0, bytes_accessed=6 << 20
        ),
        name="local_back",
    )(
        send,
        recv,
        w_edge,
        w_send,
        w_recv,
        d_node,
        neighbour_send_lists,
        row(coarse_rows),
        d_pre,
        edge_cot,
    )

    node_grad = pl.pallas_call(
        combine_kernel,
        out_shape=shape((own, width), BF),
        in_specs=vmem(6),
        out_specs=vmem(1)[0],
        name="combine",
    )(here(node_sum), here(near_hit), here(far_back.reshape(-1, width)), *returned)
    return new_nodes, new_edges, node_grad, edge_grad


def solution(mesh):
    rows = P(("groups", "patch"), None)
    placed = (
        (rows,) * 4
        + (P(),) * 13
        + (
            P("patch"),
            P("patch"),
            P("patch", None),
            P("patch"),
            P("patch", None, None),
            P("patch"),
        )
    )
    return jax.shard_map(
        local,
        mesh=mesh,
        in_specs=placed,
        out_specs=(rows,) * 4,
        check_vma=False,
    )
```
